512 devices in a mesh: wide: 64 (over y, z_lo, core), narrow: 8 (over x, z_hi).
Axes of the slice: x: 4, y: 4, z: 16 (z_hi: 2, z_lo: 8; z = z_hi * 8 + z_lo), core: 2. Of those that a mesh axis runs over, the one named last changes fastest.
Arguments:
- tensor: bfloat16 [16, 4096, 8192], P('narrow', 'wide'), may hold values from -16 to 16
- factor_a: bfloat16 [32, 4096], P(None, 'wide'), may hold values from -0.21875 to 0.21875
- factor_b: bfloat16 [32, 8192], P(None, 'wide'), may hold values from -0.15625 to 0.15625
- factor_c: bfloat16 [32, 16], P(None, 'narrow'), may hold values from -4 to 4
Outputs:
- step_a: float32 [32, 4096], P(None, 'wide')
- step_b: float32 [32, 8192], P(None, 'wide')
- step_c: float32 [32, 16], P(None, 'narrow')
The draws below stay inside these ranges and needn't reach their ends.
All inputs are finite; a program needn't handle non-finite values.
Results may differ from the reference program's by a relative error of at most 0.0029.
Values may be sent and summed in bfloat16 or wider, within the bound.
No kernel may reach another device: no remote copies, remote signals or barrier semaphores. Data moves between devices by JAX's collectives and lax.ppermute only.
A program may use at most 64 MiB of HBM per device.

```python
import jax
import jax.numpy as jnp
from jax import lax

R = 32
ITERS = 2
I = 4096
J = 8192
K = 16


def spiked(array, own_key, source, target, blocks, factor):
    def block_of(position):
        return (jnp.arange(array.shape[position]) // (array.shape[position] // blocks)).reshape((-1,) + (1,) * (array.ndim - 1 - position))

    one_side = jax.random.permutation(own_key, blocks)[block_of(target)]
    second = (block_of(target) + blocks // 2) % blocks
    return jnp.where((block_of(source) == one_side) | (block_of(source) == second), factor * array, array)


def block_levels(key, dims, pieces, low, top_value):
    def one(axis_at, blocks):
        steps = jax.random.uniform(jax.random.fold_in(jax.random.fold_in(key, 6), axis_at), (blocks,), jnp.float32, low / len(pieces), top_value / len(pieces))
        return jnp.repeat(jnp.exp(steps), dims[axis_at] // blocks).reshape((-1,) + (1,) * (len(dims) - axis_at - 1))

    factor_of = one(*pieces[0])
    for cut in pieces[1:]:
        factor_of = factor_of * one(*cut)
    return factor_of


def gaussian(key, extent, deviation, reach, cuts=(), held_as=jnp.bfloat16):
    array = jax.random.normal(key, extent, jnp.float32) * deviation
    if len(cuts) > 0:
        array = block_levels(key, extent, cuts, -0.22, 0.18) * array
    return jnp.clip(array, min=-reach, max=reach).astype(held_as)


def heavy_noise(stream_key, extent, spread, most, cuts, heavy, kind=jnp.bfloat16):
    result = spread * jax.random.normal(stream_key, extent, jnp.float32)
    if cuts:
        result = result * block_levels(stream_key, extent, cuts, -0.22, 0.18)
    return jnp.clip(spiked(result, jax.random.fold_in(stream_key, 3), *heavy), -most, most).astype(kind)


def setup_inputs(seed: int = 0) -> dict:
    arg_keys = jax.random.split(jax.random.key(seed), 5)
    tensor = heavy_noise(arg_keys[0], (K, I, J), 1.0, 16.0, ((0, 8), (1, 64)), (1, 2, 64, 4.0))
    factor_a = gaussian(arg_keys[1], (R, I), (I // 6) ** -0.5, 0.21875, ((1, 64),))
    factor_b = gaussian(arg_keys[2], (R, J), (J // 6) ** -0.5, 0.15625, ((1, 64),))
    factor_c = gaussian(arg_keys[3], (R, K), (max(1, K // 6)) ** -0.5, 4.0, ((1, 8),))
    return dict(tensor=tensor, factor_a=factor_a, factor_b=factor_b, factor_c=factor_c)


damping = 1.0
highest = lax.Precision.HIGHEST


def matmul(left, right):
    return jnp.dot(left, right, precision=highest)


def outer_rows(left, right):
    return lax.dot_general(left, right, (((1,), (1,)), ((), ())), precision=highest)


def gram_product(factors, grams, directions):
    float_a, float_b, float_c = factors
    gram_a, gram_b, gram_c = grams
    dir_a, dir_b, dir_c = directions
    cross_a = outer_rows(float_a, dir_a)
    cross_b = outer_rows(float_b, dir_b)
    cross_c = outer_rows(float_c, dir_c)
    image_a = matmul(gram_b * gram_c, dir_a) + matmul(cross_b * gram_c + gram_b * cross_c, float_a) + damping * dir_a
    image_b = matmul(gram_a * gram_c, dir_b) + matmul(cross_a * gram_c + gram_a * cross_c, float_b) + damping * dir_b
    image_c = matmul(gram_a * gram_b, dir_c) + matmul(cross_a * gram_b + gram_a * cross_b, float_c) + damping * dir_c
    return image_a, image_b, image_c


def inner_all(left, right):
    return jnp.sum(left[0] * right[0]) + jnp.sum(left[1] * right[1]) + jnp.sum(left[2] * right[2])


def reference(tensor, factor_a, factor_b, factor_c):
    flattened = tensor.reshape(K * I, J)
    contracted = lax.dot_general(factor_b, flattened, (((1,), (1,)), ((), ())), preferred_element_type=jnp.float32).reshape(R, K, I)
    float_a = factor_a.astype(jnp.float32)
    float_b = factor_b.astype(jnp.float32)
    float_c = factor_c.astype(jnp.float32)
    mttkrp_a = jnp.einsum("rk,rki->ri", float_c, contracted, precision=highest)
    mttkrp_c = jnp.einsum("ri,rki->rk", float_a, contracted, precision=highest)
    khatri = (float_c[:, :, None] * float_a[:, None, :]).reshape(R, K * I).astype(jnp.bfloat16)
    mttkrp_b = jnp.dot(khatri, flattened, preferred_element_type=jnp.float32)
    gram_a = jnp.dot(factor_a, factor_a.T, preferred_element_type=jnp.float32)
    gram_b = jnp.dot(factor_b, factor_b.T, preferred_element_type=jnp.float32)
    gram_c = jnp.dot(factor_c, factor_c.T, preferred_element_type=jnp.float32)
    grad_a = matmul(gram_b * gram_c, float_a) - mttkrp_a
    grad_b = matmul(gram_a * gram_c, float_b) - mttkrp_b
    grad_c = matmul(gram_a * gram_b, float_c) - mttkrp_c
    factors = (float_a, float_b, float_c)
    grams = (gram_a, gram_b, gram_c)
    resid = (-grad_a, -grad_b, -grad_c)
    direction = resid
    steps = (jnp.zeros_like(grad_a), jnp.zeros_like(grad_b), jnp.zeros_like(grad_c))
    norm_now = inner_all(resid, resid)
    for iteration in range(ITERS):
        image = gram_product(factors, grams, direction)
        step_size = norm_now / inner_all(direction, image)
        steps = tuple(old + step_size * move for old, move in zip(steps, direction))
        if iteration + 1 < ITERS:
            resid = tuple(old - step_size * move for old, move in zip(resid, image))
            norm_next = inner_all(resid, resid)
            momentum = norm_next / norm_now
            direction = tuple(now + momentum * old for now, old in zip(resid, direction))
            norm_now = norm_next
    return steps[0], steps[1], steps[2]
```

```python
import functools

import jax
import jax.numpy as jnp
from jax import lax
from jax.experimental import pallas as pl
from jax.experimental.pallas import tpu as pltpu
from jax.sharding import Mesh
from jax.sharding import PartitionSpec as P

f32 = jnp.float32
bf16 = jnp.bfloat16
LANES = 128
damping = 1.0
highest = lax.Precision.HIGHEST

WIDE = (4, 8, 2)
NARROW = (4, 2)
LINKS = ("y", "z_lo")
OTHER = ("x", "z_hi")


def mul(left, right):
    return jnp.dot(left, right, precision=highest, preferred_element_type=f32)


def mul_t(left, right):
    return lax.dot_general(
        left, right, (((1,), (1,)), ((), ())), precision=highest, preferred_element_type=f32
    )


def t_mul(left, right):
    return lax.dot_general(
        left, right, (((0,), (0,)), ((), ())), precision=highest, preferred_element_type=f32
    )


def lane(rows, width):
    return lax.broadcasted_iota(jnp.int32, (rows, width), 1)


def columns_of(row_block):
    count, rank = row_block.shape
    eye = lax.broadcasted_iota(jnp.int32, (rank, rank), 0) == lane(rank, rank)
    return [
        jnp.sum(jnp.where(eye, row_block[k : k + 1, :], 0.0), axis=1, keepdims=True)
        for k in range(count)
    ]


def partial_b_kernel(peers, t_ref, a_ref, ct_ref, out_ref):
    rank, i_local = a_ref.shape
    factor_a = a_ref[...]
    float_a = factor_a.astype(f32)
    cols = columns_of(ct_ref[...].astype(f32))
    khatri = jnp.concatenate([col * float_a for col in cols], axis=1).astype(bf16)
    per = 8
    for base in range(0, 2 * peers, per):
        part = jnp.dot(
            khatri, t_ref[:, base * LANES : (base + per) * LANES], preferred_element_type=f32
        )
        for step in range(per):
            peer, core = divmod(base + step, 2)
            out_ref[core, peer * rank : (peer + 1) * rank, :] = part[
                :, step * LANES : (step + 1) * LANES
            ]
    gram_a = lax.dot_general(
        factor_a, factor_a, (((1,), (1,)), ((), ())), preferred_element_type=f32
    )
    half = rank // 2
    pad = jnp.zeros((half, LANES - rank), f32)
    for core in range(2):
        out_ref[core, peers * rank :, :] = jnp.concatenate(
            [gram_a[core * half : (core + 1) * half, :], pad], axis=1
        )


def send_links_kernel(peers, pair_ref, b_ref, out_ref):
    rank = b_ref.shape[0]
    half = rank // 2
    quarter = half // 2
    own_b = b_ref[...]
    gram = pair_ref[0, peers * rank :, :rank] + pair_ref[1, peers * rank :, :rank]
    high = gram.astype(bf16)
    low = (gram - high.astype(f32)).astype(bf16)
    packed = jnp.concatenate(
        [high[:quarter].astype(f32), low[:quarter].astype(f32), high[quarter:].astype(f32), low[quarter:].astype(f32)],
        axis=1,
    ).astype(bf16)
    for peer in range(peers):
        rows = pl.ds(peer * rank, rank)
        out_ref[peer, :rank, :] = (pair_ref[0, rows, :] + pair_ref[1, rows, :]).astype(bf16)
        out_ref[peer, rank : 2 * rank, :] = own_b
        out_ref[peer, 2 * rank :, :] = packed


def partials_kernel(peers, others, n_ref, t_ref, a_ref, ct_ref, got_ref, both_ref, out_ref, grams_ref, whole_b):
    rank, i_local = a_ref.shape
    quarter = rank // 4
    sum_b = jnp.zeros((rank, LANES), f32)
    for peer in range(peers):
        sum_b = sum_b + got_ref[peer, :rank, :].astype(f32)
    for core in range(2):
        for peer in range(peers):
            start = (peer * 2 + core) * LANES
            whole_b[:, start : start + LANES] = both_ref[core, peer, :rank, :]
    gram_rows = []
    for core in range(2):
        packed = jnp.zeros((quarter, LANES), f32)
        for peer in range(peers):
            packed = packed + both_ref[core, peer, rank:, :].astype(f32)
        gram_rows.append(packed[:, :rank] + packed[:, rank : 2 * rank])
        gram_rows.append(packed[:, 2 * rank : 3 * rank] + packed[:, 3 * rank :])
    gram_a = jnp.concatenate(gram_rows, axis=0)
    every_b = whole_b[...]
    contracted = lax.dot_general(
        every_b, t_ref[...], (((1,), (1,)), ((), ())), preferred_element_type=f32
    )
    gram_b = lax.dot_general(
        every_b, every_b, (((1,), (1,)), ((), ())), preferred_element_type=f32
    )
    grams_ref[0] = gram_a
    grams_ref[1] = gram_b
    first, second = columns_of(ct_ref[...].astype(f32))
    float_a = a_ref[...].astype(f32)
    spot = lane(rank, LANES)
    low_half = spot < i_local
    scaled = contracted * jnp.where(low_half, first, second)
    part_a = scaled + pltpu.roll(scaled, i_local, 1)
    against_a = contracted * jnp.concatenate([float_a, float_a], axis=1)
    c_first = jnp.sum(jnp.where(low_half, against_a, 0.0), axis=1, keepdims=True)
    c_second = jnp.sum(jnp.where(low_half, 0.0, against_a), axis=1, keepdims=True)
    at = i_local + 2 * n_ref[0]
    k_all = 2 * others
    tail = jnp.where(spot == at, c_first, 0.0)
    tail = jnp.where(spot == at + 1, c_second, tail)
    tail = jnp.where(spot == at + k_all, first, tail)
    tail = jnp.where(spot == at + k_all + 1, second, tail)
    second_tile = jnp.where(low_half, part_a, tail)
    for other in range(others):
        out_ref[other, :, :LANES] = sum_b
        out_ref[other, :, LANES:] = second_tile


def residual_kernel(others, got_ref, a_ref, b_ref, grams_ref, send_ref, ra_ref, rb_ref, ha_ref, hb_ref, c_ref):
    rank, i_local = a_ref.shape
    k_all = 2 * others
    total = got_ref[0]
    for other in range(1, others):
        total = total + got_ref[other]
    mttkrp_b = total[:, :LANES]
    mttkrp_a = total[:, LANES : LANES + i_local]
    part_c = total[:, LANES + i_local : LANES + i_local + k_all]
    factor_c = total[:, LANES + i_local + k_all : LANES + i_local + 2 * k_all]
    c_ref[...] = factor_c
    gram_a = grams_ref[0]
    gram_b = grams_ref[1]
    gram_c = mul_t(factor_c, factor_c)
    had_a = gram_b * gram_c
    had_b = gram_a * gram_c
    float_a = a_ref[...].astype(f32)
    float_b = b_ref[...].astype(f32)
    res_a = mttkrp_a - mul(had_a, float_a)
    res_b = mttkrp_b - mul(had_b, float_b)
    once_a = mul(had_a, res_a)
    once_b = mul(had_b, res_b)
    twice_a = mul(had_a, once_a)
    twice_b = mul(had_b, once_b)
    ra_ref[...] = res_a
    rb_ref[...] = res_b
    ha_ref[...] = once_a
    hb_ref[...] = once_b

    def inner(left_a, right_a, left_b, right_b):
        by_row = jnp.sum(left_a * right_a, axis=1, keepdims=True) + jnp.sum(
            left_b * right_b, axis=1, keepdims=True
        )
        return by_row

    sums = [
        inner(res_a, res_a, res_b, res_b),
        inner(res_a, once_a, res_b, once_b),
        inner(once_a, once_a, once_b, once_b),
        inner(once_a, twice_a, once_b, twice_b),
    ]
    cross_a = mul_t(float_a, res_a)
    cross_b = mul_t(float_b, res_b)
    used = 2 * rank + k_all
    base = jnp.concatenate(
        [cross_a, cross_b, part_c, jnp.zeros((rank, LANES - used), f32)], axis=1
    )
    spot = lane(rank, LANES)
    for k, value in enumerate(sums):
        base = jnp.where(spot == used + k, value, base)
    send_ref[...] = base


def step_kernel(others, n_ref, all_ref, a_ref, b_ref, grams_ref, ra_ref, rb_ref, ha_ref, hb_ref, c_ref, sa_ref, sb_ref, sc_ref):
    rank, i_local = a_ref.shape
    k_all = 2 * others
    used = 2 * rank + k_all
    every = all_ref[...]
    cross_a = every[:, :rank]
    cross_b = every[:, rank : 2 * rank]
    mttkrp_c = every[:, 2 * rank : used]
    gram_a = grams_ref[0]
    gram_b = grams_ref[1]
    factor_c = c_ref[...]
    gram_c = mul_t(factor_c, factor_c)
    had_a = gram_b * gram_c
    had_b = gram_a * gram_c
    had_c = gram_a * gram_b
    res_c = mttkrp_c - mul(had_c, factor_c)
    once_c = mul(had_c, res_c)
    twice_c = mul(had_c, once_c)
    cross_c = mul_t(factor_c, res_c)

    def total(value):
        return jnp.sum(jnp.sum(value, axis=1, keepdims=True), axis=0, keepdims=True)

    own = [
        total(res_c * res_c),
        total(res_c * once_c),
        total(once_c * once_c),
        total(once_c * twice_c),
    ]
    p0, p1, p2, p3 = [
        total(every[:, used + k : used + k + 1]) + own[k] for k in range(4)
    ]

    def mixed(xa, xb, xc):
        return (
            xb * gram_c + gram_b * xc,
            xa * gram_c + gram_a * xc,
            xa * gram_b + gram_a * xb,
        )

    eye = (
        lax.broadcasted_iota(jnp.int32, (rank, rank), 0) == lane(rank, rank)
    ).astype(f32)
    grams = (gram_a, gram_b, gram_c)
    shifted = tuple(had + damping * eye for had in (had_a, had_b, had_c))
    crosses = (cross_a, cross_b, cross_c)
    mix = mixed(*crosses)
    mix_gram = [mul(m, g) for m, g in zip(mix, grams)]
    turned = [mul_t(s, x) for s, x in zip(shifted, crosses)]
    twice_turned = [mul(s, t) for s, t in zip(shifted, turned)]
    shifted_mix = [mul(s, m) for s, m in zip(shifted, mix)]
    image_cross_t = [t + mg for t, mg in zip(turned, mix_gram)]
    image_cross = [
        mul(x, s) + mul_t(g, m) for x, s, g, m in zip(crosses, shifted, grams, mix)
    ]
    image_mix = mixed(*image_cross)
    one = damping
    c0 = p0
    k1 = p1 + one * p0
    k2 = p2 + 2.0 * one * p1 + one * one * p0
    k3 = p3 + 3.0 * one * p2 + 3.0 * one * one * p1 + one * one * one * p0
    c1 = k1
    c2 = k2
    c3 = k3
    crosses_t = [mul_t(eye, x) for x in crosses]
    c1 = c1 + total(sum(m * xt for m, xt in zip(mix, crosses_t)))
    c2 = c2 + total(
        sum(2.0 * m * t + mg * m for m, t, mg in zip(mix, turned, mix_gram))
    )
    c3 = c3 + total(
        sum(
            2.0 * m * tt + mg * sm + im * ict
            for m, tt, mg, sm, im, ict in zip(
                mix, twice_turned, mix_gram, shifted_mix, image_mix, image_cross_t
            )
        )
    )
    alpha = c0 / c1
    fresh = c0 - 2.0 * alpha * c1 + alpha * alpha * c2
    beta = fresh / c0
    keep = 1.0 + beta
    curvature = keep * keep * c1 - 2.0 * keep * alpha * c2 + alpha * alpha * c3
    second = fresh / curvature
    on_res = alpha + second * keep
    on_image = -second * alpha
    float_a = a_ref[...].astype(f32)
    float_b = b_ref[...].astype(f32)
    res_a = ra_ref[...]
    res_b = rb_ref[...]
    image_a = damping * res_a + ha_ref[...] + mul(mix[0], float_a)
    image_b = damping * res_b + hb_ref[...] + mul(mix[1], float_b)
    image_c = damping * res_c + once_c + mul(mix[2], factor_c)
    sa_ref[...] = on_res * res_a + on_image * image_a
    sb_ref[...] = on_res * res_b + on_image * image_b
    step_c = on_res * res_c + on_image * image_c
    at = 2 * n_ref[0]
    spot = lane(rank, k_all)
    square = lax.broadcasted_iota(jnp.int32, (rank, rank), 0) == lane(rank, rank)
    for k in range(2):
        column = jnp.sum(jnp.where(spot == at + k, step_c, 0.0), axis=1, keepdims=True)
        sc_ref[k : k + 1, :] = jnp.sum(jnp.where(square, column, 0.0), axis=0, keepdims=True)


def call(kernel, out_shape, operands, scalar=False, scratch=()):
    vmem = pl.BlockSpec(memory_space=pltpu.VMEM)
    specs = [vmem] * len(operands)
    if scalar:
        specs[0] = pl.BlockSpec(memory_space=pltpu.SMEM)
    outs = out_shape if isinstance(out_shape, tuple) else (out_shape,)
    result = pl.pallas_call(
        kernel,
        out_shape=outs,
        in_specs=specs,
        out_specs=tuple(vmem for _ in outs),
        scratch_shapes=list(scratch),
    )(*operands)
    return result if isinstance(out_shape, tuple) else result[0]


def on_device(tensor, factor_a, factor_b, factor_c):
    k_local, i_local, j_whole = tensor.shape
    rank = factor_a.shape[0]
    peers = j_whole // (2 * LANES)
    others = lax.axis_size(OTHER)
    like = jax.ShapeDtypeStruct
    flattened = tensor.reshape(k_local * i_local, j_whole)
    turned_c = factor_c.T
    own = lax.axis_index(OTHER).astype(jnp.int32).reshape(1)
    half = rank // 2

    pair = call(
        functools.partial(partial_b_kernel, peers),
        like((2, peers * rank + half, LANES), f32),
        (flattened, factor_a, turned_c),
    )
    pair = lax.all_to_all(pair, "core", 0, 0, tiled=True)
    links = call(
        functools.partial(send_links_kernel, peers),
        like((peers, 2 * rank + rank // 4, LANES), bf16),
        (pair, factor_b),
    )
    links = lax.all_to_all(links, LINKS, 0, 0, tiled=True)
    both = lax.all_gather(links[:, rank:, :], "core", axis=0, tiled=False)
    narrow, grams = call(
        functools.partial(partials_kernel, peers, others),
        (like((others, rank, 2 * LANES), f32), like((2, rank, rank), f32)),
        (own, flattened, factor_a, turned_c, links, both),
        scalar=True,
        scratch=(pltpu.VMEM((rank, j_whole), bf16),),
    )
    narrow = lax.all_to_all(narrow, OTHER, 0, 0, tiled=True)
    square = like((rank, LANES), f32)
    thin = like((rank, i_local), f32)
    send, res_a, res_b, once_a, once_b, whole_c = call(
        functools.partial(residual_kernel, others),
        (square, thin, square, thin, square, like((rank, 2 * others), f32)),
        (narrow, factor_a, factor_b, grams),
    )
    send = lax.psum(send, "core")
    send = lax.dynamic_slice_in_dim(send, lax.axis_index("core") * half, half, 0)
    send = jnp.broadcast_to(send, (peers, half, LANES))
    send = lax.all_to_all(send, LINKS, 0, 0, tiled=True)
    every = lax.all_gather(jnp.sum(send, axis=0), "core", axis=0, tiled=True)
    step_a, step_b, turned_step_c = call(
        functools.partial(step_kernel, others),
        (thin, square, like((k_local, rank), f32)),
        (own, every, factor_a, factor_b, grams, res_a, res_b, once_a, once_b, whole_c),
        scalar=True,
    )
    return step_a, step_b, turned_step_c.T


def solution(mesh):
    inner = Mesh(
        mesh.devices.reshape(WIDE + NARROW), ("y", "z_lo", "core", "x", "z_hi")
    )
    wide = ("y", "z_lo", "core")
    return jax.shard_map(
        on_device,
        mesh=inner,
        in_specs=(P(OTHER, wide, None), P(None, wide), P(None, wide), P(None, OTHER)),
        out_specs=(P(None, wide), P(None, wide), P(None, OTHER)),
        check_vma=False,
    )
```

```python
import functools

import jax
import jax.numpy as jnp
from jax import lax
from jax.experimental import pallas as pl
from jax.experimental.pallas import tpu as pltpu
from jax.sharding import Mesh
from jax.sharding import PartitionSpec as P

f32 = jnp.float32
bf16 = jnp.bfloat16
LANES = 128
damping = 1.0
highest = lax.Precision.HIGHEST

WIDE = (4, 8, 2)
NARROW = (4, 2)
LINKS = ("y", "z_lo")
OTHER = ("x", "z_hi")


def mul(left, right):
    return jnp.dot(left, right, precision=highest, preferred_element_type=f32)


def mul_t(left, right):
    return lax.dot_general(
        left, right, (((1,), (1,)), ((), ())), precision=highest, preferred_element_type=f32
    )


def t_mul(left, right):
    return lax.dot_general(
        left, right, (((0,), (0,)), ((), ())), precision=highest, preferred_element_type=f32
    )


def lane(rows, width):
    return lax.broadcasted_iota(jnp.int32, (rows, width), 1)


def columns_of(row_block):
    count, rank = row_block.shape
    eye = lax.broadcasted_iota(jnp.int32, (rank, rank), 0) == lane(rank, rank)
    return [
        jnp.sum(jnp.where(eye, row_block[k : k + 1, :], 0.0), axis=1, keepdims=True)
        for k in range(count)
    ]


def spread(square):
    rows = square.shape[0] // 4
    return jnp.concatenate([square[k * rows : (k + 1) * rows, :] for k in range(4)], axis=1)


def gather_rows(wide_block):
    width = wide_block.shape[1] // 4
    return jnp.concatenate([wide_block[:, k * width : (k + 1) * width] for k in range(4)], axis=0)


def partial_b_kernel(peers, place_ref, t_ref, a_ref, ct_ref, keep_ref, send_ref):
    rank, i_local = a_ref.shape
    half = rank // 2
    factor_a = a_ref[...]
    float_a = factor_a.astype(f32)
    cols = columns_of(ct_ref[...].astype(f32))
    khatri = jnp.concatenate([col * float_a for col in cols], axis=1).astype(bf16)
    first_core = place_ref[0] % 2 == 0

    def put(rows, even, odd):
        keep_ref[rows, :] = jnp.where(first_core, even, odd)
        send_ref[rows, :] = jnp.where(first_core, odd, even)

    per = 8
    for base in range(0, 2 * peers, per):
        part = jnp.dot(
            khatri, t_ref[:, base * LANES : (base + per) * LANES], preferred_element_type=f32
        )
        for step in range(0, per, 2):
            peer = (base + step) // 2
            put(
                pl.ds(peer * rank, rank),
                part[:, step * LANES : (step + 1) * LANES],
                part[:, (step + 1) * LANES : (step + 2) * LANES],
            )
    gram = lax.dot_general(
        factor_a, factor_a, (((1,), (1,)), ((), ())), preferred_element_type=f32
    )
    gram = jnp.concatenate([gram, jnp.zeros((rank, LANES - rank), f32)], axis=1)
    put(pl.ds(peers * rank, half), gram[:half], gram[half:])


def send_links_kernel(peers, keep_ref, came_ref, b_ref, out_ref):
    rank = b_ref.shape[0]
    quarter = rank // 4
    own_b = b_ref[...]
    last = pl.ds(peers * rank, 2 * quarter)
    gram = keep_ref[last, :rank] + came_ref[last, :rank]
    high = gram.astype(bf16).astype(f32)
    low = gram - high
    packed = jnp.concatenate(
        [high[:quarter], low[:quarter], high[quarter:], low[quarter:]], axis=1
    ).astype(bf16)
    for peer in range(peers):
        rows = pl.ds(peer * rank, rank)
        out_ref[peer, :rank, :] = (keep_ref[rows, :] + came_ref[rows, :]).astype(bf16)
        out_ref[peer, rank : 2 * rank, :] = own_b
        out_ref[peer, 2 * rank :, :] = packed


def partials_kernel(peers, others, place_ref, t_ref, a_ref, ct_ref, got_ref, both_ref, out_ref, grams_ref, whole_b):
    rank, i_local = a_ref.shape
    quarter = rank // 4
    sum_b = got_ref[0, :rank, :].astype(f32)
    for peer in range(1, peers):
        sum_b = sum_b + got_ref[peer, :rank, :].astype(f32)
    gram_rows = []
    for core in range(2):
        packed = jnp.zeros((quarter, LANES), f32)
        for peer in range(peers):
            start = (peer * 2 + core) * LANES
            whole_b[:, start : start + LANES] = both_ref[core, peer, :rank, :]
            packed = packed + both_ref[core, peer, rank:, :].astype(f32)
        gram_rows.append(packed[:, :rank] + packed[:, rank : 2 * rank])
        gram_rows.append(packed[:, 2 * rank : 3 * rank] + packed[:, 3 * rank :])
    every_b = whole_b[...]
    contracted = lax.dot_general(
        every_b, t_ref[...], (((1,), (1,)), ((), ())), preferred_element_type=f32
    )
    grams_ref[0] = jnp.concatenate(gram_rows, axis=0)
    grams_ref[1] = lax.dot_general(
        every_b, every_b, (((1,), (1,)), ((), ())), preferred_element_type=f32
    )
    first, second = columns_of(ct_ref[...].astype(f32))
    float_a = a_ref[...].astype(f32)
    spot = lane(rank, LANES)
    low_half = spot < i_local
    scaled = contracted * jnp.where(low_half, first, second)
    part_a = scaled + pltpu.roll(scaled, i_local, 1)
    against_a = contracted * jnp.concatenate([float_a, float_a], axis=1)
    c_first = jnp.sum(jnp.where(low_half, against_a, 0.0), axis=1, keepdims=True)
    c_second = jnp.sum(jnp.where(low_half, 0.0, against_a), axis=1, keepdims=True)
    at = i_local + 2 * (place_ref[0] // 2)
    k_all = 2 * others
    tail = jnp.where(spot == at, c_first, 0.0)
    tail = jnp.where(spot == at + 1, c_second, tail)
    tail = jnp.where(spot == at + k_all, first, tail)
    tail = jnp.where(spot == at + k_all + 1, second, tail)
    tile = jnp.where(low_half, part_a, tail)
    for other in range(others):
        out_ref[other, :, :LANES] = sum_b
        out_ref[other, :, LANES:] = tile


def residual_kernel(others, place_ref, got_ref, a_ref, b_ref, grams_ref, send_ref, second_ref, ra_ref, rb_ref, ha_ref, hb_ref, c_ref):
    rank, i_local = a_ref.shape
    k_all = 2 * others
    total = got_ref[0]
    for other in range(1, others):
        total = total + got_ref[other]
    mttkrp_b = total[:, :LANES]
    mttkrp_a = total[:, LANES : LANES + i_local]
    part_c = total[:, LANES + i_local : LANES + i_local + k_all]
    factor_c = total[:, LANES + i_local + k_all : LANES + i_local + 2 * k_all]
    c_ref[...] = factor_c
    gram_a = grams_ref[0]
    gram_b = grams_ref[1]
    gram_c = mul_t(factor_c, factor_c)
    had_a = gram_b * gram_c
    had_b = gram_a * gram_c
    float_a = a_ref[...].astype(f32)
    float_b = b_ref[...].astype(f32)
    res_a = mttkrp_a - mul(had_a, float_a)
    res_b = mttkrp_b - mul(had_b, float_b)
    once_a = mul(had_a, res_a)
    once_b = mul(had_b, res_b)
    twice_a = mul(had_a, once_a)
    twice_b = mul(had_b, once_b)
    ra_ref[...] = res_a
    rb_ref[...] = res_b
    ha_ref[...] = once_a
    hb_ref[...] = once_b

    def inner(left_a, right_a, left_b, right_b):
        by_row = jnp.sum(left_a * right_a, axis=1, keepdims=True) + jnp.sum(
            left_b * right_b, axis=1, keepdims=True
        )
        return by_row

    sums = [
        inner(res_a, res_a, res_b, res_b),
        inner(res_a, once_a, res_b, once_b),
        inner(once_a, once_a, once_b, once_b),
        inner(once_a, twice_a, once_b, twice_b),
    ]
    cross_a = mul_t(float_a, res_a)
    cross_b = mul_t(float_b, res_b)
    last = jnp.concatenate(
        [part_c, *sums, jnp.zeros((rank, rank - k_all - len(sums)), f32)], axis=1
    )
    second_ref[...] = jnp.zeros(second_ref.shape, f32) + (place_ref[0] % 2).astype(f32)
    send_ref[0] = spread(cross_a)
    send_ref[1] = spread(cross_b)
    send_ref[2] = spread(last)


def step_kernel(others, place_ref, all_ref, a_ref, b_ref, grams_ref, ra_ref, rb_ref, ha_ref, hb_ref, c_ref, sa_ref, sb_ref, sc_ref):
    rank, i_local = a_ref.shape
    k_all = 2 * others
    cross_a = gather_rows(all_ref[0])
    cross_b = gather_rows(all_ref[1])
    last = gather_rows(all_ref[2])
    mttkrp_c = last[:, :k_all]
    gram_a = grams_ref[0]
    gram_b = grams_ref[1]
    factor_c = c_ref[...]
    gram_c = mul_t(factor_c, factor_c)
    had_a = gram_b * gram_c
    had_b = gram_a * gram_c
    had_c = gram_a * gram_b
    res_c = mttkrp_c - mul(had_c, factor_c)
    once_c = mul(had_c, res_c)
    twice_c = mul(had_c, once_c)
    cross_c = mul_t(factor_c, res_c)

    def total(value):
        return jnp.sum(jnp.sum(value, axis=1, keepdims=True), axis=0, keepdims=True)

    own = [
        total(res_c * res_c),
        total(res_c * once_c),
        total(once_c * once_c),
        total(once_c * twice_c),
    ]
    p0, p1, p2, p3 = [
        total(last[:, k_all + k : k_all + k + 1]) + own[k] for k in range(4)
    ]

    def mixed(xa, xb, xc):
        return (
            xb * gram_c + gram_b * xc,
            xa * gram_c + gram_a * xc,
            xa * gram_b + gram_a * xb,
        )

    eye = (
        lax.broadcasted_iota(jnp.int32, (rank, rank), 0) == lane(rank, rank)
    ).astype(f32)
    grams = (gram_a, gram_b, gram_c)
    shifted = tuple(had + damping * eye for had in (had_a, had_b, had_c))
    crosses = (cross_a, cross_b, cross_c)
    mix = mixed(*crosses)
    mix_gram = [mul(m, g) for m, g in zip(mix, grams)]
    turned = [mul_t(s, x) for s, x in zip(shifted, crosses)]
    twice_turned = [mul(s, t) for s, t in zip(shifted, turned)]
    shifted_mix = [mul(s, m) for s, m in zip(shifted, mix)]
    image_cross_t = [t + mg for t, mg in zip(turned, mix_gram)]
    image_cross = [
        mul(x, s) + mul_t(g, m) for x, s, g, m in zip(crosses, shifted, grams, mix)
    ]
    image_mix = mixed(*image_cross)
    one = damping
    c0 = p0
    k1 = p1 + one * p0
    k2 = p2 + 2.0 * one * p1 + one * one * p0
    k3 = p3 + 3.0 * one * p2 + 3.0 * one * one * p1 + one * one * one * p0
    c1 = k1
    c2 = k2
    c3 = k3
    crosses_t = [mul_t(eye, x) for x in crosses]
    c1 = c1 + total(sum(m * xt for m, xt in zip(mix, crosses_t)))
    c2 = c2 + total(
        sum(2.0 * m * t + mg * m for m, t, mg in zip(mix, turned, mix_gram))
    )
    c3 = c3 + total(
        sum(
            2.0 * m * tt + mg * sm + im * ict
            for m, tt, mg, sm, im, ict in zip(
                mix, twice_turned, mix_gram, shifted_mix, image_mix, image_cross_t
            )
        )
    )
    alpha = c0 / c1
    fresh = c0 - 2.0 * alpha * c1 + alpha * alpha * c2
    beta = fresh / c0
    keep = 1.0 + beta
    curvature = keep * keep * c1 - 2.0 * keep * alpha * c2 + alpha * alpha * c3
    second = fresh / curvature
    on_res = alpha + second * keep
    on_image = -second * alpha
    float_a = a_ref[...].astype(f32)
    float_b = b_ref[...].astype(f32)
    res_a = ra_ref[...]
    res_b = rb_ref[...]
    image_a = damping * res_a + ha_ref[...] + mul(mix[0], float_a)
    image_b = damping * res_b + hb_ref[...] + mul(mix[1], float_b)
    image_c = damping * res_c + once_c + mul(mix[2], factor_c)
    sa_ref[...] = on_res * res_a + on_image * image_a
    sb_ref[...] = on_res * res_b + on_image * image_b
    step_c = on_res * res_c + on_image * image_c
    at = 2 * (place_ref[0] // 2)
    spot = lane(rank, k_all)
    square = lax.broadcasted_iota(jnp.int32, (rank, rank), 0) == lane(rank, rank)
    for k in range(2):
        column = jnp.sum(jnp.where(spot == at + k, step_c, 0.0), axis=1, keepdims=True)
        sc_ref[k : k + 1, :] = jnp.sum(jnp.where(square, column, 0.0), axis=0, keepdims=True)


def call(kernel, out_shape, operands, scalar=False, scratch=(), room=16):
    vmem = pl.BlockSpec(memory_space=pltpu.VMEM)
    specs = [vmem] * len(operands)
    if scalar:
        specs[0] = pl.BlockSpec(memory_space=pltpu.SMEM)
    outs = out_shape if isinstance(out_shape, tuple) else (out_shape,)
    result = pl.pallas_call(
        kernel,
        out_shape=outs,
        in_specs=specs,
        out_specs=tuple(vmem for _ in outs),
        scratch_shapes=list(scratch),
        compiler_params=pltpu.CompilerParams(vmem_limit_bytes=room << 20),
    )(*operands)
    return result if isinstance(out_shape, tuple) else result[0]


def on_device(tensor, factor_a, factor_b, factor_c):
    k_local, i_local, j_whole = tensor.shape
    rank = factor_a.shape[0]
    peers = j_whole // (2 * LANES)
    others = lax.axis_size(OTHER)
    like = jax.ShapeDtypeStruct
    flattened = tensor.reshape(k_local * i_local, j_whole)
    turned_c = factor_c.T
    place = (lax.axis_index("core") + 2 * lax.axis_index(OTHER)).astype(jnp.int32).reshape(1)
    half = rank // 2

    rows = like((peers * rank + half, LANES), f32)
    keep, send = call(
        functools.partial(partial_b_kernel, peers),
        (rows, rows),
        (place, flattened, factor_a, turned_c),
        scalar=True,
    )
    came = lax.ppermute(send, "core", [(0, 1), (1, 0)])
    links = call(
        functools.partial(send_links_kernel, peers),
        like((peers, 2 * rank + rank // 4, LANES), bf16),
        (keep, came, factor_b),
    )
    links = lax.all_to_all(links, LINKS, 0, 0, tiled=True)
    both = lax.all_gather(links[:, rank:, :], "core", axis=0, tiled=False)
    narrow, grams = call(
        functools.partial(partials_kernel, peers, others),
        (like((others, rank, 2 * LANES), f32), like((2, rank, rank), f32)),
        (place, flattened, factor_a, turned_c, links, both),
        scalar=True,
        scratch=(pltpu.VMEM((rank, j_whole), bf16),),
    )
    narrow = lax.all_to_all(narrow, OTHER, 0, 0, tiled=True)
    square = like((rank, LANES), f32)
    thin = like((rank, i_local), f32)
    send, second, res_a, res_b, once_a, once_b, whole_c = call(
        functools.partial(residual_kernel, others),
        (like((3, 8, LANES), f32), like((4, LANES), f32), thin, square, thin, square, like((rank, 2 * others), f32)),
        (place, narrow, factor_a, factor_b, grams),
        scalar=True,
    )
    send = lax.psum(send, "core").reshape(6, 4, LANES)
    send = jnp.where(second > 0.5, send[3:], send[:3])
    send = jnp.broadcast_to(send, (peers, 3, 4, LANES))
    send = lax.all_to_all(send, LINKS, 0, 0, tiled=True)
    every = lax.all_gather(jnp.sum(send, axis=0), "core", axis=0, tiled=True)
    step_a, step_b, turned_step_c = call(
        functools.partial(step_kernel, others),
        (thin, square, like((k_local, rank), f32)),
        (place, every.reshape(3, 8, LANES), factor_a, factor_b, grams, res_a, res_b, once_a, once_b, whole_c),
        scalar=True,
    )
    return step_a, step_b, turned_step_c.T


def solution(mesh):
    inner = Mesh(
        mesh.devices.reshape(WIDE + NARROW), ("y", "z_lo", "core", "x", "z_hi")
    )
    wide = ("y", "z_lo", "core")
    return jax.shard_map(
        on_device,
        mesh=inner,
        in_specs=(P(OTHER, wide, None), P(None, wide), P(None, wide), P(None, OTHER)),
        out_specs=(P(None, wide), P(None, wide), P(None, OTHER)),
        check_vma=False,
    )
```

```python
import functools

import jax
import jax.numpy as jnp
from jax import lax
from jax.experimental import pallas as pl
from jax.experimental.pallas import tpu as pltpu
from jax.sharding import Mesh
from jax.sharding import PartitionSpec as P


f32 = jnp.float32
bf16 = jnp.bfloat16
LANES = 128
damping = 1.0
highest = lax.Precision.HIGHEST

WIDE = (4, 2, 4, 2)
NARROW = (4, 2)
NEAR = ("y", "z_near")
LINKS = ("y", "z_far", "z_near")
OTHER = ("x", "z_hi")


def mul(left, right):
    return jnp.dot(left, right, precision=highest, preferred_element_type=f32)


def mul_t(left, right):
    return lax.dot_general(
        left, right, (((1,), (1,)), ((), ())), precision=highest, preferred_element_type=f32
    )


def lane(rows, width):
    return lax.broadcasted_iota(jnp.int32, (rows, width), 1)


def columns_of(row_block):
    count, rank = row_block.shape
    eye = lax.broadcasted_iota(jnp.int32, (rank, rank), 0) == lane(rank, rank)
    return [
        jnp.sum(jnp.where(eye, row_block[k : k + 1, :], 0.0), axis=1, keepdims=True)
        for k in range(count)
    ]


def spread(square):
    rows = square.shape[0] // 4
    return jnp.concatenate([square[k * rows : (k + 1) * rows, :] for k in range(4)], axis=1)


def gather_rows(wide_block):
    width = wide_block.shape[1] // 4
    return jnp.concatenate([wide_block[:, k * width : (k + 1) * width] for k in range(4)], axis=0)


def share_kernel(a_hbm, b_hbm, ct_hbm, own_ref, khatri_ref, a_ref, b_ref, ct_ref, sems):
    copies = [
        pltpu.make_async_copy(source, target, sems.at[k])
        for k, (source, target) in enumerate(((a_hbm, a_ref), (b_hbm, b_ref), (ct_hbm, ct_ref)))
    ]
    for copy in copies:
        copy.start()
    for copy in copies:
        copy.wait()
    rank = a_ref.shape[0]
    factor_a = a_ref[...]
    own_ref[:rank, :] = b_ref[...]
    own_ref[rank:, :] = two_terms(
        lax.dot_general(
            factor_a, factor_a, (((1,), (1,)), ((), ())), preferred_element_type=f32
        )
    )
    float_a = factor_a.astype(f32)
    cols = columns_of(ct_ref[...].astype(f32))
    khatri_ref[...] = jnp.concatenate([col * float_a for col in cols], axis=1).astype(bf16)


def two_terms(square):
    half = square.shape[0] // 2
    high = square.astype(bf16).astype(f32)
    low = square - high
    return jnp.concatenate([high[:half], high[half:], low[:half], low[half:]], axis=1).astype(bf16)


def one_square(packed):
    width = packed.shape[1] // 4
    return jnp.concatenate(
        [
            packed[:, :width] + packed[:, 2 * width : 3 * width],
            packed[:, width : 2 * width] + packed[:, 3 * width :],
        ],
        axis=0,
    )


def partial_b_kernel(place_ref, khatri_ref, t_ref, keep_ref, send_ref):
    khatri = khatri_ref[...]
    pieces = 4
    width = t_ref.shape[1] // pieces
    first_core = place_ref[0] % 2 == 0
    per = width // LANES
    for piece in range(pieces):
        part = jnp.dot(
            khatri, t_ref[:, piece * width : (piece + 1) * width], preferred_element_type=f32
        )
        for step in range(0, per, 2):
            chunk = (piece * per + step) // 2
            even = part[:, step * LANES : (step + 1) * LANES]
            odd = part[:, (step + 1) * LANES : (step + 2) * LANES]
            keep_ref[chunk] = jnp.where(first_core, even, odd)
            send_ref[chunk] = jnp.where(first_core, odd, even)


def send_near_kernel(nears, place_ref, keep_ref, came_ref, own_ref, far_ref, out_ref):
    rank = keep_ref.shape[1]
    near_z = WIDE[2]
    first_far = (place_ref[0] // 2) % 2 == 0
    own_b = own_ref[:rank, :]
    far_b = far_ref[:rank, :]
    low_b = jnp.where(first_far, own_b.astype(f32), far_b.astype(f32)).astype(bf16)
    high_b = jnp.where(first_far, far_b.astype(f32), own_b.astype(f32)).astype(bf16)
    gram = two_terms(
        one_square(own_ref[rank:, :].astype(f32)) + one_square(far_ref[rank:, :].astype(f32))
    )
    for near in range(nears):
        y, z = divmod(near, near_z)
        for far in range(2):
            chunk = (y * 2 + far) * near_z + z
            out_ref[near, far * rank : (far + 1) * rank, :] = (
                keep_ref[chunk] + came_ref[chunk]
            ).astype(bf16)
        out_ref[near, 2 * rank : 3 * rank, :] = low_b
        out_ref[near, 3 * rank : 4 * rank, :] = high_b
        out_ref[near, 4 * rank :, :] = gram


def sum_b_kernel(nears, place_ref, got_ref, keep_ref, send_ref):
    rank = keep_ref.shape[0]
    first_far = (place_ref[0] // 2) % 2 == 0
    sums = []
    for far in range(2):
        rows = pl.ds(far * rank, rank)
        total = got_ref[0, rows, :].astype(f32)
        for near in range(1, nears):
            total = total + got_ref[near, rows, :].astype(f32)
        sums.append(total)
    keep_ref[...] = jnp.where(first_far, sums[0], sums[1])
    send_ref[...] = jnp.where(first_far, sums[1], sums[0])


def partials_kernel(nears, others, place_ref, t_ref, a_ref, ct_ref, both_ref, tile_ref, grams_ref, whole_b):
    rank, i_local = a_ref.shape
    near_z = WIDE[2]
    packed = jnp.zeros((rank // 2, LANES), f32)
    for core in range(2):
        for near in range(nears):
            y, z = divmod(near, near_z)
            for far in range(2):
                start = (((y * 2 + far) * near_z + z) * 2 + core) * LANES
                whole_b[:, start : start + LANES] = both_ref[
                    core, near, far * rank : (far + 1) * rank, :
                ]
            packed = packed + both_ref[core, near, 2 * rank :, :].astype(f32)
    every_b = whole_b[...]
    contracted = lax.dot_general(
        every_b, t_ref[...], (((1,), (1,)), ((), ())), preferred_element_type=f32
    )
    grams_ref[0] = one_square(packed)
    grams_ref[1] = lax.dot_general(
        every_b, every_b, (((1,), (1,)), ((), ())), preferred_element_type=f32
    )
    first, second = columns_of(ct_ref[...].astype(f32))
    float_a = a_ref[...].astype(f32)
    spot = lane(rank, LANES)
    low_half = spot < i_local
    scaled = contracted * jnp.where(low_half, first, second)
    part_a = scaled + pltpu.roll(scaled, i_local, 1)
    against_a = contracted * jnp.concatenate([float_a, float_a], axis=1)
    c_first = jnp.sum(jnp.where(low_half, against_a, 0.0), axis=1, keepdims=True)
    c_second = jnp.sum(jnp.where(low_half, 0.0, against_a), axis=1, keepdims=True)
    at = i_local + 2 * (place_ref[0] // 4)
    k_all = 2 * others
    tail = jnp.where(spot == at, c_first, 0.0)
    tail = jnp.where(spot == at + 1, c_second, tail)
    tail = jnp.where(spot == at + k_all, first, tail)
    tail = jnp.where(spot == at + k_all + 1, second, tail)
    tile_ref[...] = jnp.where(low_half, part_a, tail)


def send_narrow_kernel(others, keep_ref, came_ref, tile_ref, out_ref):
    sum_b = keep_ref[...] + came_ref[...]
    tile = tile_ref[...]
    for other in range(others):
        out_ref[other, :, :LANES] = sum_b
        out_ref[other, :, LANES:] = tile


def residual_kernel(others, got_ref, a_ref, b_ref, grams_ref, send_ref, ra_ref, rb_ref, ha_ref, hb_ref, c_ref):
    rank, i_local = a_ref.shape
    k_all = 2 * others
    total = got_ref[0]
    for other in range(1, others):
        total = total + got_ref[other]
    mttkrp_b = total[:, :LANES]
    mttkrp_a = total[:, LANES : LANES + i_local]
    part_c = total[:, LANES + i_local : LANES + i_local + k_all]
    factor_c = total[:, LANES + i_local + k_all : LANES + i_local + 2 * k_all]
    c_ref[...] = factor_c
    gram_a = grams_ref[0]
    gram_b = grams_ref[1]
    gram_c = mul_t(factor_c, factor_c)
    had_a = gram_b * gram_c
    had_b = gram_a * gram_c
    float_a = a_ref[...].astype(f32)
    float_b = b_ref[...].astype(f32)
    res_a = mttkrp_a - mul(had_a, float_a)
    res_b = mttkrp_b - mul(had_b, float_b)
    once_a = mul(had_a, res_a)
    once_b = mul(had_b, res_b)
    twice_a = mul(had_a, once_a)
    twice_b = mul(had_b, once_b)
    ra_ref[...] = res_a
    rb_ref[...] = res_b
    ha_ref[...] = once_a
    hb_ref[...] = once_b

    def inner(left_a, right_a, left_b, right_b):
        by_row = jnp.sum(left_a * right_a, axis=1, keepdims=True) + jnp.sum(
            left_b * right_b, axis=1, keepdims=True
        )
        return by_row

    sums = [
        inner(res_a, res_a, res_b, res_b),
        inner(res_a, once_a, res_b, once_b),
        inner(once_a, once_a, once_b, once_b),
        inner(once_a, twice_a, once_b, twice_b),
    ]
    cross_a = mul_t(float_a, res_a)
    cross_b = mul_t(float_b, res_b)
    last = jnp.concatenate(
        [part_c, *sums, jnp.zeros((rank, rank - k_all - len(sums)), f32)], axis=1
    )
    send_ref[0] = spread(cross_a)
    send_ref[1] = spread(cross_b)
    send_ref[2] = spread(last)


def send_links_kernel(links, place_ref, pair_ref, out_ref):
    first_core = place_ref[0] % 2 == 0
    last = pair_ref[2]
    high = last.astype(bf16).astype(f32)
    cross = jnp.where(first_core, pair_ref[0], pair_ref[1])
    tail = jnp.where(first_core, high, last - high)
    packed = jnp.concatenate([cross, tail], axis=0).astype(bf16)
    for link in range(links):
        out_ref[link] = packed


def step_kernel(others, place_ref, all_ref, a_ref, b_ref, grams_ref, ra_ref, rb_ref, ha_ref, hb_ref, c_ref, sa_ref, sb_ref, sc_ref):
    rank, _ = a_ref.shape
    k_all = 2 * others
    sums = []
    for core in range(2):
        total_sum = all_ref[core, 0].astype(f32)
        for link in range(1, all_ref.shape[1]):
            total_sum = total_sum + all_ref[core, link].astype(f32)
        sums.append(total_sum)
    slab = rank // 4
    cross_a = gather_rows(sums[0][:slab])
    cross_b = gather_rows(sums[1][:slab])
    last = gather_rows(sums[0][slab:] + sums[1][slab:])
    mttkrp_c = last[:, :k_all]
    gram_a = grams_ref[0]
    gram_b = grams_ref[1]
    factor_c = c_ref[...]
    gram_c = mul_t(factor_c, factor_c)
    had_a = gram_b * gram_c
    had_b = gram_a * gram_c
    had_c = gram_a * gram_b
    res_c = mttkrp_c - mul(had_c, factor_c)
    once_c = mul(had_c, res_c)
    twice_c = mul(had_c, once_c)
    cross_c = mul_t(factor_c, res_c)

    def total(value):
        return jnp.sum(jnp.sum(value, axis=1, keepdims=True), axis=0, keepdims=True)

    own = [
        total(res_c * res_c),
        total(res_c * once_c),
        total(once_c * once_c),
        total(once_c * twice_c),
    ]
    p0, p1, p2, p3 = [
        total(last[:, k_all + k : k_all + k + 1]) + own[k] for k in range(4)
    ]

    def mixed(xa, xb, xc):
        return (
            xb * gram_c + gram_b * xc,
            xa * gram_c + gram_a * xc,
            xa * gram_b + gram_a * xb,
        )

    eye = (
        lax.broadcasted_iota(jnp.int32, (rank, rank), 0) == lane(rank, rank)
    ).astype(f32)
    grams = (gram_a, gram_b, gram_c)
    shifted = tuple(had + damping * eye for had in (had_a, had_b, had_c))
    crosses = (cross_a, cross_b, cross_c)
    mix = mixed(*crosses)
    mix_gram = [mul(m, g) for m, g in zip(mix, grams)]
    turned = [mul_t(s, x) for s, x in zip(shifted, crosses)]
    twice_turned = [mul(s, t) for s, t in zip(shifted, turned)]
    shifted_mix = [mul(s, m) for s, m in zip(shifted, mix)]
    image_cross_t = [t + mg for t, mg in zip(turned, mix_gram)]
    image_cross = [
        mul(x, s) + mul_t(g, m) for x, s, g, m in zip(crosses, shifted, grams, mix)
    ]
    image_mix = mixed(*image_cross)
    one = damping
    c0 = p0
    k1 = p1 + one * p0
    k2 = p2 + 2.0 * one * p1 + one * one * p0
    k3 = p3 + 3.0 * one * p2 + 3.0 * one * one * p1 + one * one * one * p0
    c1 = k1
    c2 = k2
    c3 = k3
    crosses_t = [mul_t(eye, x) for x in crosses]
    c1 = c1 + total(sum(m * xt for m, xt in zip(mix, crosses_t)))
    c2 = c2 + total(
        sum(2.0 * m * t + mg * m for m, t, mg in zip(mix, turned, mix_gram))
    )
    c3 = c3 + total(
        sum(
            2.0 * m * tt + mg * sm + im * ict
            for m, tt, mg, sm, im, ict in zip(
                mix, twice_turned, mix_gram, shifted_mix, image_mix, image_cross_t
            )
        )
    )
    alpha = c0 / c1
    fresh = c0 - 2.0 * alpha * c1 + alpha * alpha * c2
    beta = fresh / c0
    keep = 1.0 + beta
    curvature = keep * keep * c1 - 2.0 * keep * alpha * c2 + alpha * alpha * c3
    second = fresh / curvature
    on_res = alpha + second * keep
    on_image = -second * alpha
    float_a = a_ref[...].astype(f32)
    float_b = b_ref[...].astype(f32)
    res_a = ra_ref[...]
    res_b = rb_ref[...]
    image_a = damping * res_a + ha_ref[...] + mul(mix[0], float_a)
    image_b = damping * res_b + hb_ref[...] + mul(mix[1], float_b)
    image_c = damping * res_c + once_c + mul(mix[2], factor_c)
    sa_ref[...] = on_res * res_a + on_image * image_a
    sb_ref[...] = on_res * res_b + on_image * image_b
    step_c = on_res * res_c + on_image * image_c
    at = 2 * (place_ref[0] // 4)
    spot = lane(rank, k_all)
    square = lax.broadcasted_iota(jnp.int32, (rank, rank), 0) == lane(rank, rank)
    for k in range(2):
        column = jnp.sum(jnp.where(spot == at + k, step_c, 0.0), axis=1, keepdims=True)
        sc_ref[k : k + 1, :] = jnp.sum(jnp.where(square, column, 0.0), axis=0, keepdims=True)


VMEM_BYTES = 67043328


def call(kernel, out_shape, operands, scalar=False, scratch=(), limit=16 << 20, fetch=()):
    vmem = pl.BlockSpec(memory_space=pltpu.VMEM)
    specs = [vmem] * len(operands)
    for k in fetch:
        specs[k] = pl.BlockSpec(memory_space=pltpu.HBM)
    if scalar:
        specs[0] = pl.BlockSpec(memory_space=pltpu.SMEM)
    outs = out_shape if isinstance(out_shape, tuple) else (out_shape,)
    result = pl.pallas_call(
        kernel,
        out_shape=outs,
        in_specs=specs,
        out_specs=tuple(vmem for _ in outs),
        scratch_shapes=list(scratch),
        compiler_params=pltpu.CompilerParams(vmem_limit_bytes=limit),
    )(*operands)
    return result if isinstance(out_shape, tuple) else result[0]


def stages(tensor, factor_a, factor_b, factor_c):
    k_local, i_local, j_whole = tensor.shape
    rank = factor_a.shape[0]
    chunks = j_whole // (2 * LANES)
    nears = chunks // 2
    others = lax.axis_size(OTHER)
    like = jax.ShapeDtypeStruct
    flattened = tensor.reshape(k_local * i_local, j_whole)
    turned_c = factor_c.T
    place = (
        lax.axis_index("core") + 2 * lax.axis_index("z_far") + 4 * lax.axis_index(OTHER)
    ).astype(jnp.int32).reshape(1)
    half = rank // 2
    square = like((rank, LANES), f32)
    thin = like((rank, i_local), f32)

    own, khatri = call(
        share_kernel,
        (like((rank + half, LANES), bf16), like((rank, k_local * i_local), bf16)),
        (factor_a, factor_b, turned_c),
        scratch=(
            pltpu.VMEM(factor_a.shape, bf16),
            pltpu.VMEM(factor_b.shape, bf16),
            pltpu.VMEM(turned_c.shape, bf16),
            pltpu.SemaphoreType.DMA((3,)),
        ),
        limit=VMEM_BYTES,
        fetch=(0, 1, 2),
    )
    far = lax.ppermute(own, "z_far", [(0, 1), (1, 0)])
    block = like((chunks, rank, LANES), f32)
    keep, send = call(
        partial_b_kernel,
        (block, block),
        (place, khatri, flattened),
        scalar=True,
    )
    came = lax.ppermute(send, "core", [(0, 1), (1, 0)])
    near = call(
        functools.partial(send_near_kernel, nears),
        like((nears, 4 * rank + half, LANES), bf16),
        (place, keep, came, own, far),
        scalar=True,
    )
    near = lax.all_to_all(near, NEAR, 0, 0, tiled=True)
    keep, send = call(
        functools.partial(sum_b_kernel, nears), (square, square), (place, near), scalar=True
    )
    came = lax.ppermute(send, "z_far", [(0, 1), (1, 0)])
    both = lax.all_gather(near[:, 2 * rank :, :], "core", axis=0, tiled=False)
    tile, grams = call(
        functools.partial(partials_kernel, nears, others),
        (square, like((2, rank, rank), f32)),
        (place, flattened, factor_a, turned_c, both),
        scalar=True,
        scratch=(pltpu.VMEM((rank, j_whole), bf16),),
    )
    narrow = call(
        functools.partial(send_narrow_kernel, others),
        like((others, rank, 2 * LANES), f32),
        (keep, came, tile),
    )
    narrow = lax.all_to_all(narrow, OTHER, 0, 0, tiled=True)
    send, res_a, res_b, once_a, once_b, whole_c = call(
        functools.partial(residual_kernel, others),
        (like((3, 8, LANES), f32), thin, square, thin, square, like((rank, 2 * others), f32)),
        (narrow, factor_a, factor_b, grams),
    )
    send = lax.psum(send, "core")
    send = call(
        functools.partial(send_links_kernel, chunks),
        like((chunks, half, LANES), bf16),
        (place, send),
        scalar=True,
    )
    send = lax.all_to_all(send, LINKS, 0, 0, tiled=True)
    every = lax.all_gather(send, "core", axis=0, tiled=False)
    step_a, step_b, turned_step_c = call(
        functools.partial(step_kernel, others),
        (thin, square, like((k_local, rank), f32)),
        (place, every, factor_a, factor_b, grams, res_a, res_b, once_a, once_b, whole_c),
        scalar=True,
    )
    return step_a, step_b, turned_step_c.T


def solution(mesh):
    wide = ("y", "z_far", "z_near", "core")
    inner = Mesh(mesh.devices.reshape(WIDE + NARROW), wide + OTHER)
    return jax.shard_map(
        stages,
        mesh=inner,
        in_specs=(P(OTHER, wide, None), P(None, wide), P(None, wide), P(None, OTHER)),
        out_specs=(P(None, wide), P(None, wide), P(None, OTHER)),
        check_vma=False,
    )
```

```python
import functools

import jax
import jax.numpy as jnp
from jax import lax
from jax.experimental import pallas as pl
from jax.experimental.pallas import tpu as pltpu
from jax.sharding import Mesh
from jax.sharding import PartitionSpec as P


f32 = jnp.float32
bf16 = jnp.bfloat16
LANES = 128
damping = 1.0
highest = lax.Precision.HIGHEST

WIDE = (4, 2, 4, 2)
NARROW = (4, 2)
NEAR = ("y", "z_near")
LINKS = ("y", "z_far", "z_near")
OTHER = ("x", "z_hi")


def mul(left, right):
    return jnp.dot(left, right, precision=highest, preferred_element_type=f32)


def mul_t(left, right):
    return lax.dot_general(
        left, right, (((1,), (1,)), ((), ())), precision=highest, preferred_element_type=f32
    )


def lane(rows, width):
    return lax.broadcasted_iota(jnp.int32, (rows, width), 1)


def columns_of(row_block):
    count, rank = row_block.shape
    eye = lax.broadcasted_iota(jnp.int32, (rank, rank), 0) == lane(rank, rank)
    return [
        jnp.sum(jnp.where(eye, row_block[k : k + 1, :], 0.0), axis=1, keepdims=True)
        for k in range(count)
    ]


def spread(square):
    rows = square.shape[0] // 4
    return jnp.concatenate([square[k * rows : (k + 1) * rows, :] for k in range(4)], axis=1)


def gather_rows(wide_block):
    width = wide_block.shape[1] // 4
    return jnp.concatenate([wide_block[:, k * width : (k + 1) * width] for k in range(4)], axis=0)


def partial_b_kernel(chunks, place_ref, t_ref, a_ref, ct_ref, keep_ref, send_ref):
    rank, _ = a_ref.shape
    factor_a = a_ref[...]
    float_a = factor_a.astype(f32)
    cols = columns_of(ct_ref[...].astype(f32))
    khatri = jnp.concatenate([col * float_a for col in cols], axis=1).astype(bf16)
    pieces = 4
    width = t_ref.shape[1] // pieces
    first_core = place_ref[0] % 2 == 0
    per = width // LANES
    for piece in range(pieces):
        part = jnp.dot(
            khatri, t_ref[:, piece * width : (piece + 1) * width], preferred_element_type=f32
        )
        for step in range(0, per, 2):
            rows = pl.ds((piece * per + step) // 2 * rank, rank)
            even = part[:, step * LANES : (step + 1) * LANES]
            odd = part[:, (step + 1) * LANES : (step + 2) * LANES]
            keep_ref[rows, :] = jnp.where(first_core, even, odd)
            send_ref[rows, :] = jnp.where(first_core, odd, even)
    gram = spread(
        lax.dot_general(
            factor_a, factor_a, (((1,), (1,)), ((), ())), preferred_element_type=f32
        )
    )
    keep_ref[chunks * rank :, :] = gram
    send_ref[chunks * rank :, :] = gram


def send_near_kernel(nears, place_ref, keep_ref, came_ref, own_ref, far_ref, out_ref):
    rank = own_ref.shape[0]
    near_z = WIDE[2]
    first_far = (place_ref[0] // 2) % 2 == 0
    own_b = own_ref[...].astype(f32)
    far_b = far_ref[...].astype(f32)
    low_b = jnp.where(first_far, own_b, far_b).astype(bf16)
    high_b = jnp.where(first_far, far_b, own_b).astype(bf16)
    last = pl.ds(2 * nears * rank, rank // 4)
    gram = keep_ref[last, :] + came_ref[last, :]
    lead = gram.astype(bf16).astype(f32)
    terms = jnp.concatenate([lead, gram - lead], axis=0).astype(bf16)
    for near in range(nears):
        y, z = divmod(near, near_z)
        for far in range(2):
            rows = pl.ds(((y * 2 + far) * near_z + z) * rank, rank)
            out_ref[near, far * rank : (far + 1) * rank, :] = (
                keep_ref[rows, :] + came_ref[rows, :]
            ).astype(bf16)
        out_ref[near, 2 * rank : 3 * rank, :] = low_b
        out_ref[near, 3 * rank : 4 * rank, :] = high_b
        out_ref[near, 4 * rank :, :] = terms


def sum_b_kernel(nears, place_ref, got_ref, a_ref, b_ref, keep_ref, send_ref, factors_ref):
    rank, _ = a_ref.shape
    slab = rank // 4
    first_far = (place_ref[0] // 2) % 2 == 0

    def summed(rows):
        total = got_ref[0, rows, :].astype(f32)
        for near in range(1, nears):
            total = total + got_ref[near, rows, :].astype(f32)
        return total

    low, high = summed(pl.ds(0, rank)), summed(pl.ds(rank, rank))
    terms = summed(pl.ds(4 * rank, 2 * slab))
    gram = terms[:slab] + terms[slab:]
    keep_ref[:rank, :] = jnp.where(first_far, low, high)
    send_ref[:rank, :] = jnp.where(first_far, high, low)
    keep_ref[rank:, :] = gram
    send_ref[rank:, :] = gram
    float_a = a_ref[...].astype(f32)
    factors_ref[:, :LANES] = b_ref[...]
    factors_ref[:, LANES:] = jnp.concatenate([float_a, float_a], axis=1).astype(bf16)


def partials_kernel(nears, others, place_ref, t_ref, a_ref, ct_ref, both_ref, tile_ref, gram_ref, whole_b):
    rank, i_local = a_ref.shape
    near_z = WIDE[2]
    for core in range(2):
        for near in range(nears):
            y, z = divmod(near, near_z)
            for far in range(2):
                start = (((y * 2 + far) * near_z + z) * 2 + core) * LANES
                whole_b[:, start : start + LANES] = both_ref[
                    core, near, far * rank : (far + 1) * rank, :
                ]
    every_b = whole_b[...]
    contracted = lax.dot_general(
        every_b, t_ref[...], (((1,), (1,)), ((), ())), preferred_element_type=f32
    )
    gram_ref[...] = lax.dot_general(
        every_b, every_b, (((1,), (1,)), ((), ())), preferred_element_type=f32
    )
    first, second = columns_of(ct_ref[...].astype(f32))
    float_a = a_ref[...].astype(f32)
    spot = lane(rank, LANES)
    low_half = spot < i_local
    scaled = contracted * jnp.where(low_half, first, second)
    part_a = scaled + pltpu.roll(scaled, i_local, 1)
    against_a = contracted * jnp.concatenate([float_a, float_a], axis=1)
    c_first = jnp.sum(jnp.where(low_half, against_a, 0.0), axis=1, keepdims=True)
    c_second = jnp.sum(jnp.where(low_half, 0.0, against_a), axis=1, keepdims=True)
    at = i_local + 2 * (place_ref[0] // 4)
    k_all = 2 * others
    tail = jnp.where(spot == at, c_first, 0.0)
    tail = jnp.where(spot == at + 1, c_second, tail)
    tail = jnp.where(spot == at + k_all, first, tail)
    tail = jnp.where(spot == at + k_all + 1, second, tail)
    tile_ref[...] = jnp.where(low_half, part_a, tail)


def send_narrow_kernel(others, keep_ref, came_ref, tile_ref, factors_ref, out_ref, gram_ref):
    rank = tile_ref.shape[0]
    total = keep_ref[...] + came_ref[...]
    gram_ref[...] = gather_rows(total[rank:])
    sum_b = total[:rank]
    tile = tile_ref[...]
    for other in range(others):
        out_ref[other, :, :LANES] = sum_b
        out_ref[other, :, LANES:] = tile


def residual_kernel(others, links, place_ref, got_ref, factors_ref, gram_a_ref, gram_b_ref, out_ref, ra_ref, rb_ref, ha_ref, hb_ref, c_ref):
    rank, i_local = ra_ref.shape
    k_all = 2 * others
    first_core = place_ref[0] % 2 == 0
    gram_a = gram_a_ref[...]
    gram_b = gram_b_ref[...]
    totals = []
    for core in range(2):
        total = got_ref[core, 0]
        for other in range(1, others):
            total = total + got_ref[core, other]
        totals.append(total)
    after = LANES + i_local
    factor_c = totals[0][:, after + k_all : after + 2 * k_all]
    part_c = totals[0][:, after : after + k_all] + totals[1][:, after : after + k_all]
    gram_c = mul_t(factor_c, factor_c)
    had_a = gram_b * gram_c
    had_b = gram_a * gram_c
    sums = [jnp.zeros((rank, 1), f32)] * 4
    cross_a = jnp.zeros((rank, rank), f32)
    cross_b = cross_a
    kept = []
    for core in range(2):
        float_b = factors_ref[core, :, :LANES].astype(f32)
        float_a = factors_ref[core, :, LANES : LANES + i_local].astype(f32)
        own = []
        for mttkrp, factor, had in (
            (totals[core][:, LANES:after], float_a, had_a),
            (totals[core][:, :LANES], float_b, had_b),
        ):
            res = mttkrp - mul(had, factor)
            once = mul(had, res)
            twice = mul(had, once)
            own += [res, once]
            pairs = ((res, res), (res, once), (once, once), (once, twice))
            sums = [
                old + jnp.sum(left * right, axis=1, keepdims=True)
                for old, (left, right) in zip(sums, pairs)
            ]
        cross_a = cross_a + mul_t(float_a, own[0])
        cross_b = cross_b + mul_t(float_b, own[2])
        kept.append(own)
    for ref, one, two in zip((ra_ref, ha_ref, rb_ref, hb_ref), *kept):
        ref[...] = jnp.where(first_core, one, two)
    c_ref[...] = factor_c
    last = spread(
        jnp.concatenate(
            [part_c, *sums, jnp.zeros((rank, rank - k_all - len(sums)), f32)], axis=1
        )
    )
    lead = last.astype(bf16).astype(f32)
    cross = jnp.where(first_core, spread(cross_a), spread(cross_b))
    tail = jnp.where(first_core, lead, last - lead)
    packed = jnp.concatenate([cross, tail], axis=0).astype(bf16)
    for link in range(links):
        out_ref[link] = packed


def step_kernel(others, place_ref, all_ref, a_ref, b_ref, gram_a_ref, gram_b_ref, ra_ref, rb_ref, ha_ref, hb_ref, c_ref, sa_ref, sb_ref, sc_ref):
    rank, _ = a_ref.shape
    k_all = 2 * others
    sums = []
    for core in range(2):
        total_sum = all_ref[core, 0].astype(f32)
        for link in range(1, all_ref.shape[1]):
            total_sum = total_sum + all_ref[core, link].astype(f32)
        sums.append(total_sum)
    slab = rank // 4
    cross_a = gather_rows(sums[0][:slab])
    cross_b = gather_rows(sums[1][:slab])
    last = gather_rows(sums[0][slab:] + sums[1][slab:])
    mttkrp_c = last[:, :k_all]
    gram_a = gram_a_ref[...]
    gram_b = gram_b_ref[...]
    factor_c = c_ref[...]
    gram_c = mul_t(factor_c, factor_c)
    had_a = gram_b * gram_c
    had_b = gram_a * gram_c
    had_c = gram_a * gram_b
    res_c = mttkrp_c - mul(had_c, factor_c)
    once_c = mul(had_c, res_c)
    twice_c = mul(had_c, once_c)
    cross_c = mul_t(factor_c, res_c)

    def total(value):
        return jnp.sum(jnp.sum(value, axis=1, keepdims=True), axis=0, keepdims=True)

    own = [
        total(res_c * res_c),
        total(res_c * once_c),
        total(once_c * once_c),
        total(once_c * twice_c),
    ]
    p0, p1, p2, p3 = [
        total(last[:, k_all + k : k_all + k + 1]) + own[k] for k in range(4)
    ]

    def mixed(xa, xb, xc):
        return (
            xb * gram_c + gram_b * xc,
            xa * gram_c + gram_a * xc,
            xa * gram_b + gram_a * xb,
        )

    eye = (
        lax.broadcasted_iota(jnp.int32, (rank, rank), 0) == lane(rank, rank)
    ).astype(f32)
    grams = (gram_a, gram_b, gram_c)
    shifted = tuple(had + damping * eye for had in (had_a, had_b, had_c))
    crosses = (cross_a, cross_b, cross_c)
    mix = mixed(*crosses)
    mix_gram = [mul(m, g) for m, g in zip(mix, grams)]
    turned = [mul_t(s, x) for s, x in zip(shifted, crosses)]
    twice_turned = [mul(s, t) for s, t in zip(shifted, turned)]
    shifted_mix = [mul(s, m) for s, m in zip(shifted, mix)]
    image_cross_t = [t + mg for t, mg in zip(turned, mix_gram)]
    image_cross = [
        mul(x, s) + mul_t(g, m) for x, s, g, m in zip(crosses, shifted, grams, mix)
    ]
    image_mix = mixed(*image_cross)
    one = damping
    c0 = p0
    k1 = p1 + one * p0
    k2 = p2 + 2.0 * one * p1 + one * one * p0
    k3 = p3 + 3.0 * one * p2 + 3.0 * one * one * p1 + one * one * one * p0
    c1 = k1
    c2 = k2
    c3 = k3
    crosses_t = [mul_t(eye, x) for x in crosses]
    c1 = c1 + total(sum(m * xt for m, xt in zip(mix, crosses_t)))
    c2 = c2 + total(
        sum(2.0 * m * t + mg * m for m, t, mg in zip(mix, turned, mix_gram))
    )
    c3 = c3 + total(
        sum(
            2.0 * m * tt + mg * sm + im * ict
            for m, tt, mg, sm, im, ict in zip(
                mix, twice_turned, mix_gram, shifted_mix, image_mix, image_cross_t
            )
        )
    )
    alpha = c0 / c1
    fresh = c0 - 2.0 * alpha * c1 + alpha * alpha * c2
    beta = fresh / c0
    keep = 1.0 + beta
    curvature = keep * keep * c1 - 2.0 * keep * alpha * c2 + alpha * alpha * c3
    second = fresh / curvature
    on_res = alpha + second * keep
    on_image = -second * alpha
    float_a = a_ref[...].astype(f32)
    float_b = b_ref[...].astype(f32)
    res_a = ra_ref[...]
    res_b = rb_ref[...]
    image_a = damping * res_a + ha_ref[...] + mul(mix[0], float_a)
    image_b = damping * res_b + hb_ref[...] + mul(mix[1], float_b)
    image_c = damping * res_c + once_c + mul(mix[2], factor_c)
    sa_ref[...] = on_res * res_a + on_image * image_a
    sb_ref[...] = on_res * res_b + on_image * image_b
    step_c = on_res * res_c + on_image * image_c
    at = 2 * (place_ref[0] // 4)
    spot = lane(rank, k_all)
    square = lax.broadcasted_iota(jnp.int32, (rank, rank), 0) == lane(rank, rank)
    for k in range(2):
        column = jnp.sum(jnp.where(spot == at + k, step_c, 0.0), axis=1, keepdims=True)
        sc_ref[k : k + 1, :] = jnp.sum(jnp.where(square, column, 0.0), axis=0, keepdims=True)


def call(kernel, out_shape, operands, scalar=False, scratch=()):
    vmem = pl.BlockSpec(memory_space=pltpu.VMEM)
    specs = [vmem] * len(operands)
    if scalar:
        specs[0] = pl.BlockSpec(memory_space=pltpu.SMEM)
    outs = out_shape if isinstance(out_shape, tuple) else (out_shape,)
    result = pl.pallas_call(
        kernel,
        out_shape=outs,
        in_specs=specs,
        out_specs=tuple(vmem for _ in outs),
        scratch_shapes=list(scratch),
        compiler_params=pltpu.CompilerParams(vmem_limit_bytes=16 << 20),
    )(*operands)
    return result if isinstance(out_shape, tuple) else result[0]


def stages(tensor, factor_a, factor_b, factor_c):
    k_local, i_local, j_whole = tensor.shape
    rank = factor_a.shape[0]
    chunks = j_whole // (2 * LANES)
    nears = chunks // 2
    others = lax.axis_size(OTHER)
    like = jax.ShapeDtypeStruct
    flattened = tensor.reshape(k_local * i_local, j_whole)
    turned_c = factor_c.T
    place = (
        lax.axis_index("core") + 2 * lax.axis_index("z_far") + 4 * lax.axis_index(OTHER)
    ).astype(jnp.int32).reshape(1)
    half = rank // 2
    square = like((rank, LANES), f32)
    thin = like((rank, i_local), f32)

    slab = rank // 4
    far = lax.ppermute(factor_b, "z_far", [(0, 1), (1, 0)])
    rows = like((chunks * rank + slab, LANES), f32)
    keep, send = call(
        functools.partial(partial_b_kernel, chunks),
        (rows, rows),
        (place, flattened, factor_a, turned_c),
        scalar=True,
    )
    came = lax.ppermute(send, "core", [(0, 1), (1, 0)])
    near = call(
        functools.partial(send_near_kernel, nears),
        like((nears, 4 * rank + half, LANES), bf16),
        (place, keep, came, factor_b, far),
        scalar=True,
    )
    near = lax.all_to_all(near, NEAR, 0, 0, tiled=True)
    rows = like((rank + slab, LANES), f32)
    keep, send, factors = call(
        functools.partial(sum_b_kernel, nears),
        (rows, rows, like((rank, 2 * LANES), bf16)),
        (place, near, factor_a, factor_b),
        scalar=True,
    )
    came = lax.ppermute(send, "z_far", [(0, 1), (1, 0)])
    both = lax.all_gather(near[:, 2 * rank : 4 * rank, :], "core", axis=0, tiled=False)
    tile, gram_b = call(
        functools.partial(partials_kernel, nears, others),
        (square, like((rank, rank), f32)),
        (place, flattened, factor_a, turned_c, both),
        scalar=True,
        scratch=(pltpu.VMEM((rank, j_whole), bf16),),
    )
    factors = lax.all_gather(factors, "core", axis=0, tiled=False)
    narrow, gram_a = call(
        functools.partial(send_narrow_kernel, others),
        (like((others, rank, 2 * LANES), f32), like((rank, rank), f32)),
        (keep, came, tile, factors),
    )
    narrow = lax.all_to_all(narrow, OTHER, 0, 0, tiled=True)
    narrow = lax.all_gather(narrow, "core", axis=0, tiled=False)
    send, res_a, res_b, once_a, once_b, whole_c = call(
        functools.partial(residual_kernel, others, chunks),
        (like((chunks, half, LANES), bf16), thin, square, thin, square, like((rank, 2 * others), f32)),
        (place, narrow, factors, gram_a, gram_b),
        scalar=True,
    )
    send = lax.all_to_all(send, LINKS, 0, 0, tiled=True)
    every = lax.all_gather(send, "core", axis=0, tiled=False)
    step_a, step_b, turned_step_c = call(
        functools.partial(step_kernel, others),
        (thin, square, like((k_local, rank), f32)),
        (place, every, factor_a, factor_b, gram_a, gram_b, res_a, res_b, once_a, once_b, whole_c),
        scalar=True,
    )
    return step_a, step_b, turned_step_c.T


def solution(mesh):
    wide = ("y", "z_far", "z_near", "core")
    inner = Mesh(mesh.devices.reshape(WIDE + NARROW), wide + OTHER)
    return jax.shard_map(
        stages,
        mesh=inner,
        in_specs=(P(OTHER, wide, None), P(None, wide), P(None, wide), P(None, OTHER)),
        out_specs=(P(None, wide), P(None, wide), P(None, OTHER)),
        check_vma=False,
    )
```

```python
import functools

import jax
import jax.numpy as jnp
from jax import lax
from jax.experimental import pallas as pl
from jax.experimental.pallas import tpu as pltpu
from jax.sharding import Mesh
from jax.sharding import PartitionSpec as P


f32 = jnp.float32
bf16 = jnp.bfloat16
LANES = 128
damping = 1.0
highest = lax.Precision.HIGHEST

WIDE = (4, 2, 4, 2)
NARROW = (4, 2)
NEAR = ("y", "z_near")
LINKS = ("y", "z_far", "z_near")
OTHER = ("x", "z_hi")


def mul(left, right):
    return jnp.dot(left, right, precision=highest, preferred_element_type=f32)


def mul_t(left, right):
    return lax.dot_general(
        left, right, (((1,), (1,)), ((), ())), precision=highest, preferred_element_type=f32
    )


def lane(rows, width):
    return lax.broadcasted_iota(jnp.int32, (rows, width), 1)


def columns_of(row_block):
    count, rank = row_block.shape
    eye = lax.broadcasted_iota(jnp.int32, (rank, rank), 0) == lane(rank, rank)
    return [
        jnp.sum(jnp.where(eye, row_block[k : k + 1, :], 0.0), axis=1, keepdims=True)
        for k in range(count)
    ]


def spread(square):
    rows = square.shape[0] // 4
    return jnp.concatenate([square[k * rows : (k + 1) * rows, :] for k in range(4)], axis=1)


def gather_rows(wide_block):
    width = wide_block.shape[1] // 4
    return jnp.concatenate([wide_block[:, k * width : (k + 1) * width] for k in range(4)], axis=0)


def partial_b_kernel(chunks, place_ref, t_ref, a_ref, ct_ref, keep_ref, send_ref):
    rank, _ = a_ref.shape
    factor_a = a_ref[...]
    float_a = factor_a.astype(f32)
    cols = columns_of(ct_ref[...].astype(f32))
    khatri = jnp.concatenate([col * float_a for col in cols], axis=1).astype(bf16)
    pieces = 4
    width = t_ref.shape[1] // pieces
    first_core = place_ref[0] % 2 == 0
    per = width // LANES
    for piece in range(pieces):
        part = jnp.dot(
            khatri, t_ref[:, piece * width : (piece + 1) * width], preferred_element_type=f32
        )
        for step in range(0, per, 2):
            rows = pl.ds((piece * per + step) // 2 * rank, rank)
            even = part[:, step * LANES : (step + 1) * LANES]
            odd = part[:, (step + 1) * LANES : (step + 2) * LANES]
            keep_ref[rows, :] = jnp.where(first_core, even, odd)
            send_ref[rows, :] = jnp.where(first_core, odd, even)
    gram = lax.dot_general(
        factor_a, factor_a, (((1,), (1,)), ((), ())), preferred_element_type=f32
    )
    slab = rank // 4
    blocks = [gram[k * slab : (k + 1) * slab, :] for k in range(4)]
    blank = jnp.zeros((slab, 2 * rank), f32)
    even = jnp.concatenate([blocks[0], blocks[1], blank], axis=1)
    odd = jnp.concatenate([blocks[2], blocks[3], blank], axis=1)
    keep_ref[chunks * rank :, :] = jnp.where(first_core, even, odd)
    send_ref[chunks * rank :, :] = jnp.where(first_core, odd, even)


def send_near_kernel(nears, place_ref, keep_ref, came_ref, own_ref, far_ref, out_ref):
    rank = own_ref.shape[0]
    near_z = WIDE[2]
    first_far = (place_ref[0] // 2) % 2 == 0
    own_b = own_ref[...].astype(f32)
    far_b = far_ref[...].astype(f32)
    low_b = jnp.where(first_far, own_b, far_b).astype(bf16)
    high_b = jnp.where(first_far, far_b, own_b).astype(bf16)
    last = pl.ds(2 * nears * rank, rank // 4)
    gram = keep_ref[last, : 2 * rank] + came_ref[last, : 2 * rank]
    lead = gram.astype(bf16).astype(f32)
    terms = jnp.concatenate([lead, gram - lead], axis=1).astype(bf16)
    for near in range(nears):
        y, z = divmod(near, near_z)
        for far in range(2):
            rows = pl.ds(((y * 2 + far) * near_z + z) * rank, rank)
            out_ref[near, far * rank : (far + 1) * rank, :] = (
                keep_ref[rows, :] + came_ref[rows, :]
            ).astype(bf16)
        out_ref[near, 2 * rank : 3 * rank, :] = low_b
        out_ref[near, 3 * rank : 4 * rank, :] = high_b
        out_ref[near, 4 * rank :, :] = terms


def sum_b_kernel(nears, place_ref, got_ref, a_ref, b_ref, keep_ref, send_ref, factors_ref):
    rank, _ = a_ref.shape
    slab = rank // 4
    first_far = (place_ref[0] // 2) % 2 == 0

    def summed(rows):
        total = got_ref[0, rows, :].astype(f32)
        for near in range(1, nears):
            total = total + got_ref[near, rows, :].astype(f32)
        return total

    low, high = summed(pl.ds(0, rank)), summed(pl.ds(rank, rank))
    terms = summed(pl.ds(4 * rank, slab))
    gram = terms[:, : 2 * rank] + terms[:, 2 * rank :]
    gram = jnp.concatenate([gram, jnp.zeros((slab, LANES - 2 * rank), f32)], axis=1)
    keep_ref[:rank, :] = jnp.where(first_far, low, high)
    send_ref[:rank, :] = jnp.where(first_far, high, low)
    keep_ref[rank:, :] = gram
    send_ref[rank:, :] = gram
    float_a = a_ref[...].astype(f32)
    factors_ref[:, :LANES] = b_ref[...]
    factors_ref[:, LANES:] = jnp.concatenate([float_a, float_a], axis=1).astype(bf16)


def partials_kernel(nears, others, place_ref, t_ref, a_ref, ct_ref, both_ref, tile_ref, gram_ref, whole_b):
    rank, i_local = a_ref.shape
    near_z = WIDE[2]
    for core in range(2):
        for near in range(nears):
            y, z = divmod(near, near_z)
            for far in range(2):
                start = (((y * 2 + far) * near_z + z) * 2 + core) * LANES
                whole_b[:, start : start + LANES] = both_ref[
                    core, near, far * rank : (far + 1) * rank, :
                ]
    every_b = whole_b[...]
    contracted = lax.dot_general(
        every_b, t_ref[...], (((1,), (1,)), ((), ())), preferred_element_type=f32
    )
    gram_ref[...] = lax.dot_general(
        every_b, every_b, (((1,), (1,)), ((), ())), preferred_element_type=f32
    )
    first, second = columns_of(ct_ref[...].astype(f32))
    float_a = a_ref[...].astype(f32)
    spot = lane(rank, LANES)
    low_half = spot < i_local
    scaled = contracted * jnp.where(low_half, first, second)
    part_a = scaled + pltpu.roll(scaled, i_local, 1)
    against_a = contracted * jnp.concatenate([float_a, float_a], axis=1)
    c_first = jnp.sum(jnp.where(low_half, against_a, 0.0), axis=1, keepdims=True)
    c_second = jnp.sum(jnp.where(low_half, 0.0, against_a), axis=1, keepdims=True)
    at = i_local + 2 * (place_ref[0] // 4)
    k_all = 2 * others
    tail = jnp.where(spot == at, c_first, 0.0)
    tail = jnp.where(spot == at + 1, c_second, tail)
    tail = jnp.where(spot == at + k_all, first, tail)
    tail = jnp.where(spot == at + k_all + 1, second, tail)
    tile_ref[...] = jnp.where(low_half, part_a, tail)


def send_narrow_kernel(others, place_ref, keep_ref, came_ref, tile_ref, factors_ref, out_ref):
    rank = tile_ref.shape[0]
    total = keep_ref[...] + came_ref[...]
    sum_b = total[:rank]
    gram = jnp.concatenate([total[rank:, :rank], total[rank:, rank : 2 * rank]], axis=0)
    gram = jnp.where(place_ref[0] // 4 == 0, gram, 0.0)
    gram = jnp.concatenate([gram, jnp.zeros((rank // 2, rank), f32)], axis=0)
    gram = jnp.concatenate([jnp.zeros((rank, LANES - rank), f32), gram], axis=1)
    tile = tile_ref[...] + gram
    for other in range(others):
        out_ref[other, :, :LANES] = sum_b
        out_ref[other, :, LANES:] = tile


def residual_kernel(others, links, place_ref, got_ref, factors_ref, gram_b_ref, out_ref, ra_ref, rb_ref, ha_ref, hb_ref, c_ref, model_c_ref, gram_a_ref, gram_c_ref):
    rank, i_local = ra_ref.shape
    k_all = 2 * others
    first_core = place_ref[0] % 2 == 0
    gram_b = gram_b_ref[...]
    totals = []
    for core in range(2):
        total = got_ref[core, 0]
        for other in range(1, others):
            total = total + got_ref[core, other]
        totals.append(total)
    after = LANES + i_local
    factor_c = totals[0][:, after + k_all : after + 2 * k_all]
    part_c = totals[0][:, after : after + k_all] + totals[1][:, after : after + k_all]
    gram_c = mul_t(factor_c, factor_c)
    gram_a = jnp.concatenate(
        [total[: rank // 2, 2 * LANES - rank :] for total in totals], axis=0
    )
    had_a = gram_b * gram_c
    had_b = gram_a * gram_c
    gram_a_ref[...] = gram_a
    gram_c_ref[...] = gram_c
    model_c_ref[...] = mul(gram_a * gram_b, factor_c)
    sums = [jnp.zeros((rank, 1), f32)] * 4
    cross_a = jnp.zeros((rank, rank), f32)
    cross_b = cross_a
    kept = []
    for core in range(2):
        float_b = factors_ref[core, :, :LANES].astype(f32)
        float_a = factors_ref[core, :, LANES : LANES + i_local].astype(f32)
        own = []
        for mttkrp, factor, had in (
            (totals[core][:, LANES:after], float_a, had_a),
            (totals[core][:, :LANES], float_b, had_b),
        ):
            res = mttkrp - mul(had, factor)
            once = mul(had, res)
            twice = mul(had, once)
            own += [res, once]
            pairs = ((res, res), (res, once), (once, once), (once, twice))
            sums = [
                old + jnp.sum(left * right, axis=1, keepdims=True)
                for old, (left, right) in zip(sums, pairs)
            ]
        cross_a = cross_a + mul_t(float_a, own[0])
        cross_b = cross_b + mul_t(float_b, own[2])
        kept.append(own)
    for ref, one, two in zip((ra_ref, ha_ref, rb_ref, hb_ref), *kept):
        ref[...] = jnp.where(first_core, one, two)
    c_ref[...] = factor_c
    last = spread(
        jnp.concatenate(
            [part_c, *sums, jnp.zeros((rank, rank - k_all - len(sums)), f32)], axis=1
        )
    )
    lead = last.astype(bf16).astype(f32)
    cross = jnp.where(first_core, spread(cross_a), spread(cross_b))
    tail = jnp.where(first_core, lead, last - lead)
    packed = jnp.concatenate([cross, tail], axis=0).astype(bf16)
    for link in range(links):
        out_ref[link] = packed


def step_kernel(others, place_ref, all_ref, a_ref, b_ref, gram_a_ref, gram_b_ref, ra_ref, rb_ref, ha_ref, hb_ref, c_ref, model_c_ref, gram_c_ref, sa_ref, sb_ref, sc_ref):
    rank, _ = a_ref.shape
    k_all = 2 * others
    sums = []
    for core in range(2):
        total_sum = all_ref[core, 0].astype(f32)
        for link in range(1, all_ref.shape[1]):
            total_sum = total_sum + all_ref[core, link].astype(f32)
        sums.append(total_sum)
    slab = rank // 4
    cross_a = gather_rows(sums[0][:slab])
    cross_b = gather_rows(sums[1][:slab])
    last = gather_rows(sums[0][slab:] + sums[1][slab:])
    mttkrp_c = last[:, :k_all]
    gram_a = gram_a_ref[...]
    gram_b = gram_b_ref[...]
    factor_c = c_ref[...]
    gram_c = gram_c_ref[...]
    had_a = gram_b * gram_c
    had_b = gram_a * gram_c
    had_c = gram_a * gram_b
    res_c = mttkrp_c - model_c_ref[...]
    once_c = mul(had_c, res_c)
    twice_c = mul(had_c, once_c)
    cross_c = mul_t(factor_c, res_c)

    def total(value):
        return jnp.sum(jnp.sum(value, axis=1, keepdims=True), axis=0, keepdims=True)

    own = [
        total(res_c * res_c),
        total(res_c * once_c),
        total(once_c * once_c),
        total(once_c * twice_c),
    ]
    p0, p1, p2, p3 = [
        total(last[:, k_all + k : k_all + k + 1]) + own[k] for k in range(4)
    ]

    def mixed(xa, xb, xc):
        return (
            xb * gram_c + gram_b * xc,
            xa * gram_c + gram_a * xc,
            xa * gram_b + gram_a * xb,
        )

    eye = (
        lax.broadcasted_iota(jnp.int32, (rank, rank), 0) == lane(rank, rank)
    ).astype(f32)
    grams = (gram_a, gram_b, gram_c)
    shifted = tuple(had + damping * eye for had in (had_a, had_b, had_c))
    crosses = (cross_a, cross_b, cross_c)
    mix = mixed(*crosses)
    mix_gram = [mul(m, g) for m, g in zip(mix, grams)]
    turned = [mul_t(s, x) for s, x in zip(shifted, crosses)]
    twice_turned = [mul(s, t) for s, t in zip(shifted, turned)]
    shifted_mix = [mul(s, m) for s, m in zip(shifted, mix)]
    image_cross_t = [t + mg for t, mg in zip(turned, mix_gram)]
    image_cross = [
        mul(x, s) + mul_t(g, m) for x, s, g, m in zip(crosses, shifted, grams, mix)
    ]
    image_mix = mixed(*image_cross)
    one = damping
    c0 = p0
    k1 = p1 + one * p0
    k2 = p2 + 2.0 * one * p1 + one * one * p0
    k3 = p3 + 3.0 * one * p2 + 3.0 * one * one * p1 + one * one * one * p0
    c1 = k1
    c2 = k2
    c3 = k3
    crosses_t = [mul_t(eye, x) for x in crosses]
    c1 = c1 + total(sum(m * xt for m, xt in zip(mix, crosses_t)))
    c2 = c2 + total(
        sum(2.0 * m * t + mg * m for m, t, mg in zip(mix, turned, mix_gram))
    )
    c3 = c3 + total(
        sum(
            2.0 * m * tt + mg * sm + im * ict
            for m, tt, mg, sm, im, ict in zip(
                mix, twice_turned, mix_gram, shifted_mix, image_mix, image_cross_t
            )
        )
    )
    alpha = c0 / c1
    fresh = c0 - 2.0 * alpha * c1 + alpha * alpha * c2
    beta = fresh / c0
    keep = 1.0 + beta
    curvature = keep * keep * c1 - 2.0 * keep * alpha * c2 + alpha * alpha * c3
    second = fresh / curvature
    on_res = alpha + second * keep
    on_image = -second * alpha
    float_a = a_ref[...].astype(f32)
    float_b = b_ref[...].astype(f32)
    res_a = ra_ref[...]
    res_b = rb_ref[...]
    image_a = damping * res_a + ha_ref[...] + mul(mix[0], float_a)
    image_b = damping * res_b + hb_ref[...] + mul(mix[1], float_b)
    image_c = damping * res_c + once_c + mul(mix[2], factor_c)
    sa_ref[...] = on_res * res_a + on_image * image_a
    sb_ref[...] = on_res * res_b + on_image * image_b
    step_c = on_res * res_c + on_image * image_c
    at = 2 * (place_ref[0] // 4)
    spot = lane(rank, k_all)
    square = lax.broadcasted_iota(jnp.int32, (rank, rank), 0) == lane(rank, rank)
    for k in range(2):
        column = jnp.sum(jnp.where(spot == at + k, step_c, 0.0), axis=1, keepdims=True)
        sc_ref[k : k + 1, :] = jnp.sum(jnp.where(square, column, 0.0), axis=0, keepdims=True)


def call(kernel, out_shape, operands, scalar=False, scratch=()):
    vmem = pl.BlockSpec(memory_space=pltpu.VMEM)
    specs = [vmem] * len(operands)
    if scalar:
        specs[0] = pl.BlockSpec(memory_space=pltpu.SMEM)
    outs = out_shape if isinstance(out_shape, tuple) else (out_shape,)
    result = pl.pallas_call(
        kernel,
        out_shape=outs,
        in_specs=specs,
        out_specs=tuple(vmem for _ in outs),
        scratch_shapes=list(scratch),
        compiler_params=pltpu.CompilerParams(vmem_limit_bytes=16 << 20),
    )(*operands)
    return result if isinstance(out_shape, tuple) else result[0]


def stages(tensor, factor_a, factor_b, factor_c):
    k_local, i_local, j_whole = tensor.shape
    rank = factor_a.shape[0]
    chunks = j_whole // (2 * LANES)
    nears = chunks // 2
    others = lax.axis_size(OTHER)
    like = jax.ShapeDtypeStruct
    flattened = tensor.reshape(k_local * i_local, j_whole)
    turned_c = factor_c.T
    place = (
        lax.axis_index("core") + 2 * lax.axis_index("z_far") + 4 * lax.axis_index(OTHER)
    ).astype(jnp.int32).reshape(1)
    half = rank // 2
    square = like((rank, LANES), f32)
    thin = like((rank, i_local), f32)

    slab = rank // 4
    far = lax.ppermute(factor_b, "z_far", [(0, 1), (1, 0)])
    rows = like((chunks * rank + slab, LANES), f32)
    keep, send = call(
        functools.partial(partial_b_kernel, chunks),
        (rows, rows),
        (place, flattened, factor_a, turned_c),
        scalar=True,
    )
    came = lax.ppermute(send, "core", [(0, 1), (1, 0)])
    near = call(
        functools.partial(send_near_kernel, nears),
        like((nears, 4 * rank + slab, LANES), bf16),
        (place, keep, came, factor_b, far),
        scalar=True,
    )
    near = lax.all_to_all(near, NEAR, 0, 0, tiled=True)
    rows = like((rank + slab, LANES), f32)
    keep, send, factors = call(
        functools.partial(sum_b_kernel, nears),
        (rows, rows, like((rank, 2 * LANES), bf16)),
        (place, near, factor_a, factor_b),
        scalar=True,
    )
    came = lax.ppermute(send, "z_far", [(0, 1), (1, 0)])
    both = lax.all_gather(near[:, 2 * rank : 4 * rank, :], "core", axis=0, tiled=False)
    tile, gram_b = call(
        functools.partial(partials_kernel, nears, others),
        (square, like((rank, rank), f32)),
        (place, flattened, factor_a, turned_c, both),
        scalar=True,
        scratch=(pltpu.VMEM((rank, j_whole), bf16),),
    )
    factors = lax.all_gather(factors, "core", axis=0, tiled=False)
    narrow = call(
        functools.partial(send_narrow_kernel, others),
        like((others, rank, 2 * LANES), f32),
        (place, keep, came, tile, factors),
        scalar=True,
    )
    narrow = lax.all_to_all(narrow, OTHER, 0, 0, tiled=True)
    narrow = lax.all_gather(narrow, "core", axis=0, tiled=False)
    low = like((rank, 2 * others), f32)
    gram = like((rank, rank), f32)
    send, res_a, res_b, once_a, once_b, whole_c, model_c, gram_a, gram_c = call(
        functools.partial(residual_kernel, others, chunks),
        (like((chunks, half, LANES), bf16), thin, square, thin, square, low, low, gram, gram),
        (place, narrow, factors, gram_b),
        scalar=True,
    )
    send = lax.all_to_all(send, LINKS, 0, 0, tiled=True)
    every = lax.all_gather(send, "core", axis=0, tiled=False)
    step_a, step_b, turned_step_c = call(
        functools.partial(step_kernel, others),
        (thin, square, like((k_local, rank), f32)),
        (place, every, factor_a, factor_b, gram_a, gram_b, res_a, res_b, once_a, once_b, whole_c, model_c, gram_c),
        scalar=True,
    )
    return step_a, step_b, turned_step_c.T


def solution(mesh):
    wide = ("y", "z_far", "z_near", "core")
    inner = Mesh(mesh.devices.reshape(WIDE + NARROW), wide + OTHER)
    return jax.shard_map(
        stages,
        mesh=inner,
        in_specs=(P(OTHER, wide, None), P(None, wide), P(None, wide), P(None, OTHER)),
        out_specs=(P(None, wide), P(None, wide), P(None, OTHER)),
        check_vma=False,
    )
```

```python
import functools

import jax
import jax.numpy as jnp
from jax import lax
from jax.experimental import pallas as pl
from jax.experimental.pallas import tpu as pltpu
from jax.sharding import Mesh
from jax.sharding import PartitionSpec as P


f32 = jnp.float32
bf16 = jnp.bfloat16
LANES = 128
damping = 1.0
highest = lax.Precision.HIGHEST

WIDE = (4, 2, 4, 2)
NARROW = (4, 2)
NEAR = ("y", "z_near")
LINKS = ("y", "z_far", "z_near")
OTHER = ("x", "z_hi")


def mul(left, right):
    return jnp.dot(left, right, precision=highest, preferred_element_type=f32)


def mul_t(left, right):
    return lax.dot_general(
        left, right, (((1,), (1,)), ((), ())), precision=highest, preferred_element_type=f32
    )


def lane(rows, width):
    return lax.broadcasted_iota(jnp.int32, (rows, width), 1)


def columns_of(row_block):
    count, rank = row_block.shape
    eye = lax.broadcasted_iota(jnp.int32, (rank, rank), 0) == lane(rank, rank)
    return [
        jnp.sum(jnp.where(eye, row_block[k : k + 1, :], 0.0), axis=1, keepdims=True)
        for k in range(count)
    ]


def spread(square):
    rows = square.shape[0] // 4
    return jnp.concatenate([square[k * rows : (k + 1) * rows, :] for k in range(4)], axis=1)


def gather_rows(wide_block):
    width = wide_block.shape[1] // 4
    return jnp.concatenate([wide_block[:, k * width : (k + 1) * width] for k in range(4)], axis=0)


def partial_b_kernel(chunks, place_ref, t_ref, a_ref, ct_ref, keep_ref, send_ref):
    rank, _ = a_ref.shape
    factor_a = a_ref[...]
    float_a = factor_a.astype(f32)
    cols = columns_of(ct_ref[...].astype(f32))
    khatri = jnp.concatenate([col * float_a for col in cols], axis=1).astype(bf16)
    pieces = 4
    width = t_ref.shape[1] // pieces
    first_core = place_ref[0] % 2 == 0
    per = width // LANES
    for piece in range(pieces):
        part = jnp.dot(
            khatri, t_ref[:, piece * width : (piece + 1) * width], preferred_element_type=f32
        )
        for step in range(0, per, 2):
            rows = pl.ds((piece * per + step) // 2 * rank, rank)
            even = part[:, step * LANES : (step + 1) * LANES]
            odd = part[:, (step + 1) * LANES : (step + 2) * LANES]
            keep_ref[rows, :] = jnp.where(first_core, even, odd)
            send_ref[rows, :] = jnp.where(first_core, odd, even)
    gram = lax.dot_general(
        factor_a, factor_a, (((1,), (1,)), ((), ())), preferred_element_type=f32
    )
    slab = rank // 4
    blocks = [gram[k * slab : (k + 1) * slab, :] for k in range(4)]
    blank = jnp.zeros((slab, 2 * rank), f32)
    even = jnp.concatenate([blocks[0], blocks[1], blank], axis=1)
    odd = jnp.concatenate([blocks[2], blocks[3], blank], axis=1)
    keep_ref[chunks * rank :, :] = jnp.where(first_core, even, odd)
    send_ref[chunks * rank :, :] = jnp.where(first_core, odd, even)


def send_near_kernel(nears, place_ref, keep_ref, came_ref, own_ref, far_ref, out_ref):
    rank = own_ref.shape[0]
    near_z = WIDE[2]
    first_far = (place_ref[0] // 2) % 2 == 0
    own_b = own_ref[...].astype(f32)
    far_b = far_ref[...].astype(f32)
    low_b = jnp.where(first_far, own_b, far_b).astype(bf16)
    high_b = jnp.where(first_far, far_b, own_b).astype(bf16)
    last = pl.ds(2 * nears * rank, rank // 4)
    gram = keep_ref[last, : 2 * rank] + came_ref[last, : 2 * rank]
    lead = gram.astype(bf16).astype(f32)
    terms = jnp.concatenate([lead, gram - lead], axis=1).astype(bf16)
    for near in range(nears):
        y, z = divmod(near, near_z)
        for far in range(2):
            rows = pl.ds(((y * 2 + far) * near_z + z) * rank, rank)
            out_ref[near, far * rank : (far + 1) * rank, :] = (
                keep_ref[rows, :] + came_ref[rows, :]
            ).astype(bf16)
        out_ref[near, 2 * rank : 3 * rank, :] = low_b
        out_ref[near, 3 * rank : 4 * rank, :] = high_b
        out_ref[near, 4 * rank :, :] = terms


def sum_b_kernel(nears, place_ref, got_ref, a_ref, b_ref, keep_ref, send_ref, factors_ref):
    rank, _ = a_ref.shape
    slab = rank // 4
    first_far = (place_ref[0] // 2) % 2 == 0

    def summed(rows):
        total = got_ref[0, rows, :].astype(f32)
        for near in range(1, nears):
            total = total + got_ref[near, rows, :].astype(f32)
        return total

    low, high = summed(pl.ds(0, rank)), summed(pl.ds(rank, rank))
    terms = summed(pl.ds(4 * rank, slab))
    gram = terms[:, : 2 * rank] + terms[:, 2 * rank :]
    gram = jnp.concatenate([gram, jnp.zeros((slab, LANES - 2 * rank), f32)], axis=1)
    keep_ref[:rank, :] = jnp.where(first_far, low, high)
    send_ref[:rank, :] = jnp.where(first_far, high, low)
    keep_ref[rank:, :] = gram
    send_ref[rank:, :] = gram
    float_a = a_ref[...].astype(f32)
    factors_ref[:, :LANES] = b_ref[...]
    factors_ref[:, LANES:] = jnp.concatenate([float_a, float_a], axis=1).astype(bf16)


def partials_kernel(nears, t_ref, a_ref, ct_ref, both_ref, tile_ref, gram_ref, whole_b):
    rank, i_local = a_ref.shape
    near_z = WIDE[2]
    for core in range(2):
        for near in range(nears):
            y, z = divmod(near, near_z)
            for far in range(2):
                start = (((y * 2 + far) * near_z + z) * 2 + core) * LANES
                whole_b[:, start : start + LANES] = both_ref[
                    core, near, far * rank : (far + 1) * rank, :
                ]
    every_b = whole_b[...]
    contracted = lax.dot_general(
        every_b, t_ref[...], (((1,), (1,)), ((), ())), preferred_element_type=f32
    )
    gram_ref[...] = lax.dot_general(
        every_b, every_b, (((1,), (1,)), ((), ())), preferred_element_type=f32
    )
    first, second = columns_of(ct_ref[...].astype(f32))
    float_a = a_ref[...].astype(f32)
    spot = lane(rank, LANES)
    low_half = spot < i_local
    scaled = contracted * jnp.where(low_half, first, second)
    part_a = scaled + pltpu.roll(scaled, i_local, 1)
    against_a = contracted * jnp.concatenate([float_a, float_a], axis=1)
    c_first = jnp.sum(jnp.where(low_half, against_a, 0.0), axis=1, keepdims=True)
    c_second = jnp.sum(jnp.where(low_half, 0.0, against_a), axis=1, keepdims=True)
    square = lax.broadcasted_iota(jnp.int32, (rank, rank), 0) == lane(rank, rank)
    parts = [jnp.sum(jnp.where(square, c, 0.0), axis=0, keepdims=True) for c in (c_first, c_second)]
    leads = [part.astype(bf16).astype(f32) for part in parts]
    rests = [part - lead for part, lead in zip(parts, leads)]
    own_c = [ct_ref[k : k + 1, :].astype(f32) for k in range(2)]
    half = rank // 2
    tile_ref[:half, :] = jnp.where(lane(half, LANES) < i_local, part_a[:half], part_a[half:])
    tile_ref[half:, :] = jnp.concatenate(
        [
            jnp.concatenate(leads + rests, axis=1),
            jnp.concatenate(own_c + [jnp.zeros((1, 2 * rank), f32)], axis=1),
            jnp.zeros((6, LANES), f32),
        ],
        axis=0,
    )


def send_narrow_kernel(others, keep_ref, came_ref, tile_ref, factors_ref, out_ref):
    rank = factors_ref.shape[1]
    half = rank // 2
    total = keep_ref[...] + came_ref[...]
    gram = total[rank:, : 2 * rank]
    lead = gram.astype(bf16).astype(f32)
    packed = jnp.concatenate(
        [
            total[:rank],
            tile_ref[:half, :],
            jnp.concatenate([lead, gram - lead], axis=1),
            tile_ref[half:, :],
        ],
        axis=0,
    ).astype(bf16)
    for other in range(others):
        out_ref[other] = packed


def residual_kernel(others, links, place_ref, got_ref, factors_ref, gram_b_ref, out_ref, ra_ref, rb_ref, ha_ref, hb_ref, c_ref, model_c_ref, gram_a_ref, gram_c_ref):
    rank, i_local = ra_ref.shape
    k_all = 2 * others
    first_core = place_ref[0] % 2 == 0
    gram_b = gram_b_ref[...]
    half = rank // 2
    slab = rank // 4
    square = lax.broadcasted_iota(jnp.int32, (rank, rank), 0) == lane(rank, rank)
    eye = square.astype(f32)
    spot = lax.broadcasted_iota(jnp.int32, (others, LANES), 0)
    mttkrps = []
    grams = []
    part_c = jnp.zeros((k_all, rank), f32)
    for core in range(2):

        def summed(rows):
            total = got_ref[core, 0, rows, :].astype(f32)
            for other in range(1, others):
                total = total + got_ref[core, other, rows, :].astype(f32)
            return total

        wide_a = summed(pl.ds(rank, half))
        mttkrps.append(
            (
                jnp.concatenate([wide_a[:, :i_local], wide_a[:, i_local:]], axis=0),
                summed(pl.ds(0, rank)),
            )
        )
        gram = got_ref[core, 0, rank + half : rank + half + slab, :].astype(f32)
        gram = gram[:, : 2 * rank] + gram[:, 2 * rank :]
        grams += [gram[:, :rank], gram[:, rank:]]
        upper = jnp.zeros((others, LANES), f32)
        lower = upper
        for other in range(others):
            block = got_ref[core, other, rank + half + slab :, :].astype(f32)
            upper = jnp.where(spot == other, block[0:1, :], upper)
            lower = jnp.where(spot == other, block[1:2, :], lower)
        upper = upper[:, : 2 * rank] + upper[:, 2 * rank :]
        part_c = part_c + jnp.concatenate([upper[:, :rank], upper[:, rank:]], axis=0)
    factor_c = mul_t(eye, jnp.concatenate([lower[:, :rank], lower[:, rank : 2 * rank]], axis=0))
    part_c = mul_t(eye, part_c)
    gram_c = mul_t(factor_c, factor_c)
    gram_a = jnp.concatenate(grams, axis=0)
    had_a = gram_b * gram_c
    had_b = gram_a * gram_c
    gram_a_ref[...] = gram_a
    gram_c_ref[...] = gram_c
    model_c_ref[...] = mul(gram_a * gram_b, factor_c)
    sums = [jnp.zeros((rank, 1), f32)] * 4
    cross_a = jnp.zeros((rank, rank), f32)
    cross_b = cross_a
    kept = []
    for core in range(2):
        float_b = factors_ref[core, :, :LANES].astype(f32)
        float_a = factors_ref[core, :, LANES : LANES + i_local].astype(f32)
        own = []
        for mttkrp, factor, had in (
            (mttkrps[core][0], float_a, had_a),
            (mttkrps[core][1], float_b, had_b),
        ):
            res = mttkrp - mul(had, factor)
            once = mul(had, res)
            twice = mul(had, once)
            own += [res, once]
            pairs = ((res, res), (res, once), (once, once), (once, twice))
            sums = [
                old + jnp.sum(left * right, axis=1, keepdims=True)
                for old, (left, right) in zip(sums, pairs)
            ]
        cross_a = cross_a + mul_t(float_a, own[0])
        cross_b = cross_b + mul_t(float_b, own[2])
        kept.append(own)
    for ref, one, two in zip((ra_ref, ha_ref, rb_ref, hb_ref), *kept):
        ref[...] = jnp.where(first_core, one, two)
    c_ref[...] = factor_c
    last = spread(
        jnp.concatenate(
            [part_c, *sums, jnp.zeros((rank, rank - k_all - len(sums)), f32)], axis=1
        )
    )
    lead = last.astype(bf16).astype(f32)
    cross = jnp.where(first_core, spread(cross_a), spread(cross_b))
    tail = jnp.where(first_core, lead, last - lead)
    packed = jnp.concatenate([cross, tail], axis=0).astype(bf16)
    for link in range(links):
        out_ref[link] = packed


def step_kernel(others, place_ref, all_ref, a_ref, b_ref, gram_a_ref, gram_b_ref, ra_ref, rb_ref, ha_ref, hb_ref, c_ref, model_c_ref, gram_c_ref, sa_ref, sb_ref, sc_ref):
    rank, _ = a_ref.shape
    k_all = 2 * others
    sums = []
    for core in range(2):
        total_sum = all_ref[core, 0].astype(f32)
        for link in range(1, all_ref.shape[1]):
            total_sum = total_sum + all_ref[core, link].astype(f32)
        sums.append(total_sum)
    slab = rank // 4
    cross_a = gather_rows(sums[0][:slab])
    cross_b = gather_rows(sums[1][:slab])
    last = gather_rows(sums[0][slab:] + sums[1][slab:])
    mttkrp_c = last[:, :k_all]
    gram_a = gram_a_ref[...]
    gram_b = gram_b_ref[...]
    factor_c = c_ref[...]
    gram_c = gram_c_ref[...]
    had_a = gram_b * gram_c
    had_b = gram_a * gram_c
    had_c = gram_a * gram_b
    res_c = mttkrp_c - model_c_ref[...]
    once_c = mul(had_c, res_c)
    twice_c = mul(had_c, once_c)
    cross_c = mul_t(factor_c, res_c)

    def total(value):
        return jnp.sum(jnp.sum(value, axis=1, keepdims=True), axis=0, keepdims=True)

    own = [
        total(res_c * res_c),
        total(res_c * once_c),
        total(once_c * once_c),
        total(once_c * twice_c),
    ]
    p0, p1, p2, p3 = [
        total(last[:, k_all + k : k_all + k + 1]) + own[k] for k in range(4)
    ]

    def mixed(xa, xb, xc):
        return (
            xb * gram_c + gram_b * xc,
            xa * gram_c + gram_a * xc,
            xa * gram_b + gram_a * xb,
        )

    eye = (
        lax.broadcasted_iota(jnp.int32, (rank, rank), 0) == lane(rank, rank)
    ).astype(f32)
    grams = (gram_a, gram_b, gram_c)
    shifted = tuple(had + damping * eye for had in (had_a, had_b, had_c))
    crosses = (cross_a, cross_b, cross_c)
    mix = mixed(*crosses)
    mix_gram = [mul(m, g) for m, g in zip(mix, grams)]
    turned = [mul_t(s, x) for s, x in zip(shifted, crosses)]
    twice_turned = [mul(s, t) for s, t in zip(shifted, turned)]
    shifted_mix = [mul(s, m) for s, m in zip(shifted, mix)]
    image_cross_t = [t + mg for t, mg in zip(turned, mix_gram)]
    image_cross = [
        mul(x, s) + mul_t(g, m) for x, s, g, m in zip(crosses, shifted, grams, mix)
    ]
    image_mix = mixed(*image_cross)
    one = damping
    c0 = p0
    k1 = p1 + one * p0
    k2 = p2 + 2.0 * one * p1 + one * one * p0
    k3 = p3 + 3.0 * one * p2 + 3.0 * one * one * p1 + one * one * one * p0
    c1 = k1
    c2 = k2
    c3 = k3
    crosses_t = [mul_t(eye, x) for x in crosses]
    c1 = c1 + total(sum(m * xt for m, xt in zip(mix, crosses_t)))
    c2 = c2 + total(
        sum(2.0 * m * t + mg * m for m, t, mg in zip(mix, turned, mix_gram))
    )
    c3 = c3 + total(
        sum(
            2.0 * m * tt + mg * sm + im * ict
            for m, tt, mg, sm, im, ict in zip(
                mix, twice_turned, mix_gram, shifted_mix, image_mix, image_cross_t
            )
        )
    )
    alpha = c0 / c1
    fresh = c0 - 2.0 * alpha * c1 + alpha * alpha * c2
    beta = fresh / c0
    keep = 1.0 + beta
    curvature = keep * keep * c1 - 2.0 * keep * alpha * c2 + alpha * alpha * c3
    second = fresh / curvature
    on_res = alpha + second * keep
    on_image = -second * alpha
    float_a = a_ref[...].astype(f32)
    float_b = b_ref[...].astype(f32)
    res_a = ra_ref[...]
    res_b = rb_ref[...]
    image_a = damping * res_a + ha_ref[...] + mul(mix[0], float_a)
    image_b = damping * res_b + hb_ref[...] + mul(mix[1], float_b)
    image_c = damping * res_c + once_c + mul(mix[2], factor_c)
    sa_ref[...] = on_res * res_a + on_image * image_a
    sb_ref[...] = on_res * res_b + on_image * image_b
    step_c = on_res * res_c + on_image * image_c
    at = place_ref[0] // 4
    spot = lane(rank, k_all)
    square = lax.broadcasted_iota(jnp.int32, (rank, rank), 0) == lane(rank, rank)
    for k in range(2):
        column = jnp.sum(jnp.where(spot == at + k * others, step_c, 0.0), axis=1, keepdims=True)
        sc_ref[k : k + 1, :] = jnp.sum(jnp.where(square, column, 0.0), axis=0, keepdims=True)


def call(kernel, out_shape, operands, scalar=False, scratch=()):
    vmem = pl.BlockSpec(memory_space=pltpu.VMEM)
    specs = [vmem] * len(operands)
    if scalar:
        specs[0] = pl.BlockSpec(memory_space=pltpu.SMEM)
    outs = out_shape if isinstance(out_shape, tuple) else (out_shape,)
    result = pl.pallas_call(
        kernel,
        out_shape=outs,
        in_specs=specs,
        out_specs=tuple(vmem for _ in outs),
        scratch_shapes=list(scratch),
        compiler_params=pltpu.CompilerParams(vmem_limit_bytes=16 << 20),
    )(*operands)
    return result if isinstance(out_shape, tuple) else result[0]


def stages(tensor, factor_a, factor_b, factor_c):
    k_local, i_local, j_whole = tensor.shape
    rank = factor_a.shape[0]
    chunks = j_whole // (2 * LANES)
    nears = chunks // 2
    others = lax.axis_size(OTHER)
    like = jax.ShapeDtypeStruct
    flattened = tensor.reshape(k_local * i_local, j_whole)
    turned_c = factor_c.T
    place = (
        lax.axis_index("core") + 2 * lax.axis_index("z_far") + 4 * lax.axis_index(OTHER)
    ).astype(jnp.int32).reshape(1)
    half = rank // 2
    square = like((rank, LANES), f32)
    thin = like((rank, i_local), f32)

    slab = rank // 4
    far = lax.ppermute(factor_b, "z_far", [(0, 1), (1, 0)])
    rows = like((chunks * rank + slab, LANES), f32)
    keep, send = call(
        functools.partial(partial_b_kernel, chunks),
        (rows, rows),
        (place, flattened, factor_a, turned_c),
        scalar=True,
    )
    came = lax.ppermute(send, "core", [(0, 1), (1, 0)])
    near = call(
        functools.partial(send_near_kernel, nears),
        like((nears, 4 * rank + slab, LANES), bf16),
        (place, keep, came, factor_b, far),
        scalar=True,
    )
    near = lax.all_to_all(near, NEAR, 0, 0, tiled=True)
    rows = like((rank + slab, LANES), f32)
    keep, send, factors = call(
        functools.partial(sum_b_kernel, nears),
        (rows, rows, like((rank, 2 * LANES), bf16)),
        (place, near, factor_a, factor_b),
        scalar=True,
    )
    came = lax.ppermute(send, "z_far", [(0, 1), (1, 0)])
    both = lax.all_gather(near[:, 2 * rank : 4 * rank, :], "core", axis=0, tiled=False)
    tile, gram_b = call(
        functools.partial(partials_kernel, nears),
        (like((half + slab, LANES), f32), like((rank, rank), f32)),
        (flattened, factor_a, turned_c, both),
        scratch=(pltpu.VMEM((rank, j_whole), bf16),),
    )
    factors = lax.all_gather(factors, "core", axis=0, tiled=False)
    narrow = call(
        functools.partial(send_narrow_kernel, others),
        like((others, rank + half + 2 * slab, LANES), bf16),
        (keep, came, tile, factors),
    )
    narrow = lax.all_to_all(narrow, OTHER, 0, 0, tiled=True)
    narrow = lax.all_gather(narrow, "core", axis=0, tiled=False)
    low = like((rank, 2 * others), f32)
    gram = like((rank, rank), f32)
    send, res_a, res_b, once_a, once_b, whole_c, model_c, gram_a, gram_c = call(
        functools.partial(residual_kernel, others, chunks),
        (like((chunks, half, LANES), bf16), thin, square, thin, square, low, low, gram, gram),
        (place, narrow, factors, gram_b),
        scalar=True,
    )
    send = lax.all_to_all(send, LINKS, 0, 0, tiled=True)
    every = lax.all_gather(send, "core", axis=0, tiled=False)
    step_a, step_b, turned_step_c = call(
        functools.partial(step_kernel, others),
        (thin, square, like((k_local, rank), f32)),
        (place, every, factor_a, factor_b, gram_a, gram_b, res_a, res_b, once_a, once_b, whole_c, model_c, gram_c),
        scalar=True,
    )
    return step_a, step_b, turned_step_c.T


def solution(mesh):
    wide = ("y", "z_far", "z_near", "core")
    inner = Mesh(mesh.devices.reshape(WIDE + NARROW), wide + OTHER)
    return jax.shard_map(
        stages,
        mesh=inner,
        in_specs=(P(OTHER, wide, None), P(None, wide), P(None, wide), P(None, OTHER)),
        out_specs=(P(None, wide), P(None, wide), P(None, OTHER)),
        check_vma=False,
    )
```

```python
import functools

import jax
import jax.numpy as jnp
from jax import lax
from jax.experimental import pallas as pl
from jax.experimental.pallas import tpu as pltpu
from jax.sharding import Mesh
from jax.sharding import PartitionSpec as P


f32 = jnp.float32
bf16 = jnp.bfloat16
LANES = 128
damping = 1.0
highest = lax.Precision.HIGHEST

WIDE = (4, 2, 4, 2)
NARROW = (4, 2)
NEAR = ("y", "z_near")
LINKS = ("y", "z_far", "z_near")
OTHER = ("x", "z_hi")


def mul(left, right):
    return jnp.dot(left, right, precision=highest, preferred_element_type=f32)


def mul_t(left, right):
    return lax.dot_general(
        left, right, (((1,), (1,)), ((), ())), precision=highest, preferred_element_type=f32
    )


def lane(rows, width):
    return lax.broadcasted_iota(jnp.int32, (rows, width), 1)


def columns_of(row_block):
    count, rank = row_block.shape
    eye = lax.broadcasted_iota(jnp.int32, (rank, rank), 0) == lane(rank, rank)
    return [
        jnp.sum(jnp.where(eye, row_block[k : k + 1, :], 0.0), axis=1, keepdims=True)
        for k in range(count)
    ]


def spread(square):
    rows = square.shape[0] // 4
    return jnp.concatenate([square[k * rows : (k + 1) * rows, :] for k in range(4)], axis=1)


def gather_rows(wide_block):
    width = wide_block.shape[1] // 4
    return jnp.concatenate([wide_block[:, k * width : (k + 1) * width] for k in range(4)], axis=0)


def lead_kernel(place_ref, out_ref):
    out_ref[0] = place_ref[0]


def partial_b_kernel(chunks, place_ref, t_ref, a_ref, ct_ref, keep_ref, send_ref):
    rank, _ = a_ref.shape
    factor_a = a_ref[...]
    float_a = factor_a.astype(f32)
    cols = columns_of(ct_ref[...].astype(f32))
    khatri = jnp.concatenate([col * float_a for col in cols], axis=1).astype(bf16)
    pieces = 4
    width = t_ref.shape[1] // pieces
    first_core = place_ref[0] % 2 == 0
    per = width // LANES
    for piece in range(pieces):
        part = jnp.dot(
            khatri, t_ref[:, piece * width : (piece + 1) * width], preferred_element_type=f32
        )
        for step in range(0, per, 2):
            rows = pl.ds((piece * per + step) // 2 * rank, rank)
            even = part[:, step * LANES : (step + 1) * LANES]
            odd = part[:, (step + 1) * LANES : (step + 2) * LANES]
            keep_ref[rows, :] = jnp.where(first_core, even, odd)
            send_ref[rows, :] = jnp.where(first_core, odd, even)
    gram = lax.dot_general(
        factor_a, factor_a, (((1,), (1,)), ((), ())), preferred_element_type=f32
    )
    slab = rank // 4
    blocks = [gram[k * slab : (k + 1) * slab, :] for k in range(4)]
    blank = jnp.zeros((slab, 2 * rank), f32)
    even = jnp.concatenate([blocks[0], blocks[1], blank], axis=1)
    odd = jnp.concatenate([blocks[2], blocks[3], blank], axis=1)
    keep_ref[chunks * rank :, :] = jnp.where(first_core, even, odd)
    send_ref[chunks * rank :, :] = jnp.where(first_core, odd, even)


def send_near_kernel(nears, place_ref, keep_ref, came_ref, own_ref, far_ref, out_ref):
    rank = own_ref.shape[0]
    near_z = WIDE[2]
    first_far = (place_ref[0] // 2) % 2 == 0
    own_b = own_ref[...].astype(f32)
    far_b = far_ref[...].astype(f32)
    low_b = jnp.where(first_far, own_b, far_b).astype(bf16)
    high_b = jnp.where(first_far, far_b, own_b).astype(bf16)
    last = pl.ds(2 * nears * rank, rank // 4)
    gram = keep_ref[last, : 2 * rank] + came_ref[last, : 2 * rank]
    lead = gram.astype(bf16).astype(f32)
    terms = jnp.concatenate([lead, gram - lead], axis=1).astype(bf16)
    for near in range(nears):
        y, z = divmod(near, near_z)
        for far in range(2):
            rows = pl.ds(((y * 2 + far) * near_z + z) * rank, rank)
            out_ref[near, far * rank : (far + 1) * rank, :] = (
                keep_ref[rows, :] + came_ref[rows, :]
            ).astype(bf16)
        out_ref[near, 2 * rank : 3 * rank, :] = low_b
        out_ref[near, 3 * rank : 4 * rank, :] = high_b
        out_ref[near, 4 * rank :, :] = terms


def sum_b_kernel(nears, place_ref, got_ref, a_ref, b_ref, keep_ref, send_ref, factors_ref):
    rank, _ = a_ref.shape
    slab = rank // 4
    first_far = (place_ref[0] // 2) % 2 == 0

    def summed(rows):
        total = got_ref[0, rows, :].astype(f32)
        for near in range(1, nears):
            total = total + got_ref[near, rows, :].astype(f32)
        return total

    low, high = summed(pl.ds(0, rank)), summed(pl.ds(rank, rank))
    terms = summed(pl.ds(4 * rank, slab))
    gram = terms[:, : 2 * rank] + terms[:, 2 * rank :]
    gram = jnp.concatenate([gram, jnp.zeros((slab, LANES - 2 * rank), f32)], axis=1)
    keep_ref[:rank, :] = jnp.where(first_far, low, high)
    send_ref[:rank, :] = jnp.where(first_far, high, low)
    keep_ref[rank:, :] = gram
    send_ref[rank:, :] = gram
    float_a = a_ref[...].astype(f32)
    factors_ref[:, :LANES] = b_ref[...]
    factors_ref[:, LANES:] = jnp.concatenate([float_a, float_a], axis=1).astype(bf16)


def partials_kernel(nears, t_ref, a_ref, ct_ref, both_ref, tile_ref, gram_ref, whole_b):
    rank, i_local = a_ref.shape
    near_z = WIDE[2]
    for core in range(2):
        for near in range(nears):
            y, z = divmod(near, near_z)
            for far in range(2):
                start = (((y * 2 + far) * near_z + z) * 2 + core) * LANES
                whole_b[:, start : start + LANES] = both_ref[
                    core, near, far * rank : (far + 1) * rank, :
                ]
    every_b = whole_b[...]
    contracted = lax.dot_general(
        every_b, t_ref[...], (((1,), (1,)), ((), ())), preferred_element_type=f32
    )
    gram_ref[...] = lax.dot_general(
        every_b, every_b, (((1,), (1,)), ((), ())), preferred_element_type=f32
    )
    first, second = columns_of(ct_ref[...].astype(f32))
    float_a = a_ref[...].astype(f32)
    spot = lane(rank, LANES)
    low_half = spot < i_local
    scaled = contracted * jnp.where(low_half, first, second)
    part_a = scaled + pltpu.roll(scaled, i_local, 1)
    against_a = contracted * jnp.concatenate([float_a, float_a], axis=1)
    c_first = jnp.sum(jnp.where(low_half, against_a, 0.0), axis=1, keepdims=True)
    c_second = jnp.sum(jnp.where(low_half, 0.0, against_a), axis=1, keepdims=True)
    square = lax.broadcasted_iota(jnp.int32, (rank, rank), 0) == lane(rank, rank)
    parts = [jnp.sum(jnp.where(square, c, 0.0), axis=0, keepdims=True) for c in (c_first, c_second)]
    leads = [part.astype(bf16).astype(f32) for part in parts]
    rests = [part - lead for part, lead in zip(parts, leads)]
    own_c = [ct_ref[k : k + 1, :].astype(f32) for k in range(2)]
    half = rank // 2
    tile_ref[:half, :] = jnp.where(lane(half, LANES) < i_local, part_a[:half], part_a[half:])
    tile_ref[half:, :] = jnp.concatenate(
        [
            jnp.concatenate(leads + rests, axis=1),
            jnp.concatenate(own_c + [jnp.zeros((1, 2 * rank), f32)], axis=1),
            jnp.zeros((6, LANES), f32),
        ],
        axis=0,
    )


def send_narrow_kernel(others, keep_ref, came_ref, tile_ref, factors_ref, out_ref):
    rank = factors_ref.shape[1]
    half = rank // 2
    total = keep_ref[...] + came_ref[...]
    gram = total[rank:, : 2 * rank]
    lead = gram.astype(bf16).astype(f32)
    packed = jnp.concatenate(
        [
            total[:rank],
            tile_ref[:half, :],
            jnp.concatenate([lead, gram - lead], axis=1),
            tile_ref[half:, :],
        ],
        axis=0,
    ).astype(bf16)
    for other in range(others):
        out_ref[other] = packed


def residual_kernel(others, links, place_ref, got_ref, factors_ref, gram_b_ref, out_ref, ra_ref, rb_ref, ha_ref, hb_ref, c_ref, model_c_ref, gram_a_ref, gram_c_ref):
    rank, i_local = ra_ref.shape
    k_all = 2 * others
    first_core = place_ref[0] % 2 == 0
    gram_b = gram_b_ref[...]
    half = rank // 2
    slab = rank // 4
    square = lax.broadcasted_iota(jnp.int32, (rank, rank), 0) == lane(rank, rank)
    eye = square.astype(f32)
    spot = lax.broadcasted_iota(jnp.int32, (others, LANES), 0)
    mttkrps = []
    grams = []
    part_c = jnp.zeros((k_all, rank), f32)
    for core in range(2):

        def summed(rows):
            total = got_ref[core, 0, rows, :].astype(f32)
            for other in range(1, others):
                total = total + got_ref[core, other, rows, :].astype(f32)
            return total

        wide_a = summed(pl.ds(rank, half))
        mttkrps.append(
            (
                jnp.concatenate([wide_a[:, :i_local], wide_a[:, i_local:]], axis=0),
                summed(pl.ds(0, rank)),
            )
        )
        gram = got_ref[core, 0, rank + half : rank + half + slab, :].astype(f32)
        gram = gram[:, : 2 * rank] + gram[:, 2 * rank :]
        grams += [gram[:, :rank], gram[:, rank:]]
        upper = jnp.zeros((others, LANES), f32)
        lower = upper
        for other in range(others):
            block = got_ref[core, other, rank + half + slab :, :].astype(f32)
            upper = jnp.where(spot == other, block[0:1, :], upper)
            lower = jnp.where(spot == other, block[1:2, :], lower)
        upper = upper[:, : 2 * rank] + upper[:, 2 * rank :]
        part_c = part_c + jnp.concatenate([upper[:, :rank], upper[:, rank:]], axis=0)
    factor_c = mul_t(eye, jnp.concatenate([lower[:, :rank], lower[:, rank : 2 * rank]], axis=0))
    part_c = mul_t(eye, part_c)
    gram_c = mul_t(factor_c, factor_c)
    gram_a = jnp.concatenate(grams, axis=0)
    had_a = gram_b * gram_c
    had_b = gram_a * gram_c
    gram_a_ref[...] = gram_a
    gram_c_ref[...] = gram_c
    model_c_ref[...] = mul(gram_a * gram_b, factor_c)
    sums = [jnp.zeros((rank, 1), f32)] * 4
    cross_a = jnp.zeros((rank, rank), f32)
    cross_b = cross_a
    kept = []
    for core in range(2):
        float_b = factors_ref[core, :, :LANES].astype(f32)
        float_a = factors_ref[core, :, LANES : LANES + i_local].astype(f32)
        own = []
        for mttkrp, factor, had in (
            (mttkrps[core][0], float_a, had_a),
            (mttkrps[core][1], float_b, had_b),
        ):
            res = mttkrp - mul(had, factor)
            once = mul(had, res)
            twice = mul(had, once)
            own += [res, once]
            pairs = ((res, res), (res, once), (once, once), (once, twice))
            sums = [
                old + jnp.sum(left * right, axis=1, keepdims=True)
                for old, (left, right) in zip(sums, pairs)
            ]
        cross_a = cross_a + mul_t(float_a, own[0])
        cross_b = cross_b + mul_t(float_b, own[2])
        kept.append(own)
    for ref, one, two in zip((ra_ref, ha_ref, rb_ref, hb_ref), *kept):
        ref[...] = jnp.where(first_core, one, two)
    c_ref[...] = factor_c
    last = spread(
        jnp.concatenate(
            [part_c, *sums, jnp.zeros((rank, rank - k_all - len(sums)), f32)], axis=1
        )
    )
    lead = last.astype(bf16).astype(f32)
    cross = jnp.where(first_core, spread(cross_a), spread(cross_b))
    tail = jnp.where(first_core, lead, last - lead)
    packed = jnp.concatenate([cross, tail], axis=0).astype(bf16)
    for link in range(links):
        out_ref[link] = packed


def step_kernel(others, place_ref, all_ref, a_ref, b_ref, gram_a_ref, gram_b_ref, ra_ref, rb_ref, ha_ref, hb_ref, c_ref, model_c_ref, gram_c_ref, sa_ref, sb_ref, sc_ref):
    rank, _ = a_ref.shape
    k_all = 2 * others
    sums = []
    for core in range(2):
        total_sum = all_ref[core, 0].astype(f32)
        for link in range(1, all_ref.shape[1]):
            total_sum = total_sum + all_ref[core, link].astype(f32)
        sums.append(total_sum)
    slab = rank // 4
    cross_a = gather_rows(sums[0][:slab])
    cross_b = gather_rows(sums[1][:slab])
    last = gather_rows(sums[0][slab:] + sums[1][slab:])
    mttkrp_c = last[:, :k_all]
    gram_a = gram_a_ref[...]
    gram_b = gram_b_ref[...]
    factor_c = c_ref[...]
    gram_c = gram_c_ref[...]
    had_a = gram_b * gram_c
    had_b = gram_a * gram_c
    had_c = gram_a * gram_b
    res_c = mttkrp_c - model_c_ref[...]
    once_c = mul(had_c, res_c)
    twice_c = mul(had_c, once_c)
    cross_c = mul_t(factor_c, res_c)

    def total(value):
        return jnp.sum(jnp.sum(value, axis=1, keepdims=True), axis=0, keepdims=True)

    own = [
        total(res_c * res_c),
        total(res_c * once_c),
        total(once_c * once_c),
        total(once_c * twice_c),
    ]
    p0, p1, p2, p3 = [
        total(last[:, k_all + k : k_all + k + 1]) + own[k] for k in range(4)
    ]

    def mixed(xa, xb, xc):
        return (
            xb * gram_c + gram_b * xc,
            xa * gram_c + gram_a * xc,
            xa * gram_b + gram_a * xb,
        )

    eye = (
        lax.broadcasted_iota(jnp.int32, (rank, rank), 0) == lane(rank, rank)
    ).astype(f32)
    grams = (gram_a, gram_b, gram_c)
    shifted = tuple(had + damping * eye for had in (had_a, had_b, had_c))
    crosses = (cross_a, cross_b, cross_c)
    mix = mixed(*crosses)
    mix_gram = [mul(m, g) for m, g in zip(mix, grams)]
    turned = [mul_t(s, x) for s, x in zip(shifted, crosses)]
    twice_turned = [mul(s, t) for s, t in zip(shifted, turned)]
    shifted_mix = [mul(s, m) for s, m in zip(shifted, mix)]
    image_cross_t = [t + mg for t, mg in zip(turned, mix_gram)]
    image_cross = [
        mul(x, s) + mul_t(g, m) for x, s, g, m in zip(crosses, shifted, grams, mix)
    ]
    image_mix = mixed(*image_cross)
    one = damping
    c0 = p0
    k1 = p1 + one * p0
    k2 = p2 + 2.0 * one * p1 + one * one * p0
    k3 = p3 + 3.0 * one * p2 + 3.0 * one * one * p1 + one * one * one * p0
    c1 = k1
    c2 = k2
    c3 = k3
    crosses_t = [mul_t(eye, x) for x in crosses]
    c1 = c1 + total(sum(m * xt for m, xt in zip(mix, crosses_t)))
    c2 = c2 + total(
        sum(2.0 * m * t + mg * m for m, t, mg in zip(mix, turned, mix_gram))
    )
    c3 = c3 + total(
        sum(
            2.0 * m * tt + mg * sm + im * ict
            for m, tt, mg, sm, im, ict in zip(
                mix, twice_turned, mix_gram, shifted_mix, image_mix, image_cross_t
            )
        )
    )
    alpha = c0 / c1
    fresh = c0 - 2.0 * alpha * c1 + alpha * alpha * c2
    beta = fresh / c0
    keep = 1.0 + beta
    curvature = keep * keep * c1 - 2.0 * keep * alpha * c2 + alpha * alpha * c3
    second = fresh / curvature
    on_res = alpha + second * keep
    on_image = -second * alpha
    float_a = a_ref[...].astype(f32)
    float_b = b_ref[...].astype(f32)
    res_a = ra_ref[...]
    res_b = rb_ref[...]
    image_a = damping * res_a + ha_ref[...] + mul(mix[0], float_a)
    image_b = damping * res_b + hb_ref[...] + mul(mix[1], float_b)
    image_c = damping * res_c + once_c + mul(mix[2], factor_c)
    sa_ref[...] = on_res * res_a + on_image * image_a
    sb_ref[...] = on_res * res_b + on_image * image_b
    step_c = on_res * res_c + on_image * image_c
    at = place_ref[0] // 4
    spot = lane(rank, k_all)
    square = lax.broadcasted_iota(jnp.int32, (rank, rank), 0) == lane(rank, rank)
    for k in range(2):
        column = jnp.sum(jnp.where(spot == at + k * others, step_c, 0.0), axis=1, keepdims=True)
        sc_ref[k : k + 1, :] = jnp.sum(jnp.where(square, column, 0.0), axis=0, keepdims=True)


def call(kernel, out_shape, operands, scalar=False, scratch=()):
    vmem = pl.BlockSpec(memory_space=pltpu.VMEM)
    specs = [vmem] * len(operands)
    if scalar:
        specs[0] = pl.BlockSpec(memory_space=pltpu.SMEM)
    outs = out_shape if isinstance(out_shape, tuple) else (out_shape,)
    result = pl.pallas_call(
        kernel,
        out_shape=outs,
        in_specs=specs,
        out_specs=tuple(vmem for _ in outs),
        scratch_shapes=list(scratch),
        compiler_params=pltpu.CompilerParams(vmem_limit_bytes=16 << 20),
    )(*operands)
    return result if isinstance(out_shape, tuple) else result[0]


def stages(tensor, factor_a, factor_b, factor_c):
    k_local, i_local, j_whole = tensor.shape
    rank = factor_a.shape[0]
    chunks = j_whole // (2 * LANES)
    nears = chunks // 2
    others = lax.axis_size(OTHER)
    like = jax.ShapeDtypeStruct
    flattened = tensor.reshape(k_local * i_local, j_whole)
    turned_c = factor_c.T
    place = (
        lax.axis_index("core") + 2 * lax.axis_index("z_far") + 4 * lax.axis_index(OTHER)
    ).astype(jnp.int32).reshape(1)
    half = rank // 2
    square = like((rank, LANES), f32)
    thin = like((rank, i_local), f32)

    slab = rank // 4
    smem = pl.BlockSpec(memory_space=pltpu.SMEM)
    place = pl.pallas_call(
        lead_kernel,
        out_shape=like((1,), jnp.int32),
        in_specs=[smem],
        out_specs=smem,
        cost_estimate=pl.CostEstimate(flops=10_000_000_000, bytes_accessed=8, transcendentals=0),
        compiler_params=pltpu.CompilerParams(vmem_limit_bytes=1 << 20),
    )(place)
    far = lax.ppermute(factor_b, "z_far", [(0, 1), (1, 0)])
    rows = like((chunks * rank + slab, LANES), f32)
    keep, send = call(
        functools.partial(partial_b_kernel, chunks),
        (rows, rows),
        (place, flattened, factor_a, turned_c),
        scalar=True,
    )
    came = lax.ppermute(send, "core", [(0, 1), (1, 0)])
    near = call(
        functools.partial(send_near_kernel, nears),
        like((nears, 4 * rank + slab, LANES), bf16),
        (place, keep, came, factor_b, far),
        scalar=True,
    )
    near = lax.all_to_all(near, NEAR, 0, 0, tiled=True)
    rows = like((rank + slab, LANES), f32)
    keep, send, factors = call(
        functools.partial(sum_b_kernel, nears),
        (rows, rows, like((rank, 2 * LANES), bf16)),
        (place, near, factor_a, factor_b),
        scalar=True,
    )
    came = lax.ppermute(send, "z_far", [(0, 1), (1, 0)])
    both = lax.all_gather(near[:, 2 * rank : 4 * rank, :], "core", axis=0, tiled=False)
    tile, gram_b = call(
        functools.partial(partials_kernel, nears),
        (like((half + slab, LANES), f32), like((rank, rank), f32)),
        (flattened, factor_a, turned_c, both),
        scratch=(pltpu.VMEM((rank, j_whole), bf16),),
    )
    factors = lax.all_gather(factors, "core", axis=0, tiled=False)
    narrow = call(
        functools.partial(send_narrow_kernel, others),
        like((others, rank + half + 2 * slab, LANES), bf16),
        (keep, came, tile, factors),
    )
    narrow = lax.all_to_all(narrow, OTHER, 0, 0, tiled=True)
    narrow = lax.all_gather(narrow, "core", axis=0, tiled=False)
    low = like((rank, 2 * others), f32)
    gram = like((rank, rank), f32)
    send, res_a, res_b, once_a, once_b, whole_c, model_c, gram_a, gram_c = call(
        functools.partial(residual_kernel, others, chunks),
        (like((chunks, half, LANES), bf16), thin, square, thin, square, low, low, gram, gram),
        (place, narrow, factors, gram_b),
        scalar=True,
    )
    send = lax.all_to_all(send, LINKS, 0, 0, tiled=True)
    every = lax.all_gather(send, "core", axis=0, tiled=False)
    step_a, step_b, turned_step_c = call(
        functools.partial(step_kernel, others),
        (thin, square, like((k_local, rank), f32)),
        (place, every, factor_a, factor_b, gram_a, gram_b, res_a, res_b, once_a, once_b, whole_c, model_c, gram_c),
        scalar=True,
    )
    return step_a, step_b, turned_step_c.T


def solution(mesh):
    wide = ("y", "z_far", "z_near", "core")
    inner = Mesh(mesh.devices.reshape(WIDE + NARROW), wide + OTHER)
    return jax.shard_map(
        stages,
        mesh=inner,
        in_specs=(P(OTHER, wide, None), P(None, wide), P(None, wide), P(None, OTHER)),
        out_specs=(P(None, wide), P(None, wide), P(None, OTHER)),
        check_vma=False,
    )
```

```python
import functools

import jax
import jax.numpy as jnp
from jax import lax
from jax.experimental import pallas as pl
from jax.experimental.pallas import tpu as pltpu
from jax.sharding import Mesh
from jax.sharding import PartitionSpec as P


f32 = jnp.float32
bf16 = jnp.bfloat16
LANES = 128
damping = 1.0
highest = lax.Precision.HIGHEST

WIDE = (4, 2, 4, 2)
NARROW = (4, 2)
NEAR = ("y", "z_near")
LINKS = ("y", "z_far", "z_near")
OTHER = ("x", "z_hi")


def mul(left, right):
    return jnp.dot(left, right, precision=highest, preferred_element_type=f32)


def mul_t(left, right):
    return lax.dot_general(
        left, right, (((1,), (1,)), ((), ())), precision=highest, preferred_element_type=f32
    )


def lane(rows, width):
    return lax.broadcasted_iota(jnp.int32, (rows, width), 1)


def columns_of(row_block):
    count, rank = row_block.shape
    eye = lax.broadcasted_iota(jnp.int32, (rank, rank), 0) == lane(rank, rank)
    return [
        jnp.sum(jnp.where(eye, row_block[k : k + 1, :], 0.0), axis=1, keepdims=True)
        for k in range(count)
    ]


def spread(square):
    rows = square.shape[0] // 4
    return jnp.concatenate([square[k * rows : (k + 1) * rows, :] for k in range(4)], axis=1)


def gather_rows(wide_block):
    width = wide_block.shape[1] // 4
    return jnp.concatenate([wide_block[:, k * width : (k + 1) * width] for k in range(4)], axis=0)


def lead_kernel(place_ref, out_ref):
    out_ref[...] = jnp.zeros(out_ref.shape, f32) + place_ref[0].astype(f32)


def partial_b_kernel(chunks, place_ref, t_ref, a_ref, ct_ref, first_ref, keep_ref, send_ref):
    rank, _ = a_ref.shape
    factor_a = a_ref[...]
    float_a = factor_a.astype(f32)
    cols = columns_of(ct_ref[...].astype(f32))
    khatri = jnp.concatenate([col * float_a for col in cols], axis=1).astype(bf16)
    pieces = 4
    width = t_ref.shape[1] // pieces
    first_core = place_ref[0] % 2 == 0
    per = width // LANES
    for piece in range(pieces):
        part = jnp.dot(
            khatri, t_ref[:, piece * width : (piece + 1) * width], preferred_element_type=f32
        )
        for step in range(0, per, 2):
            rows = pl.ds((piece * per + step) // 2 * rank, rank)
            even = part[:, step * LANES : (step + 1) * LANES]
            odd = part[:, (step + 1) * LANES : (step + 2) * LANES]
            keep_ref[rows, :] = jnp.where(first_core, even, odd)
            send_ref[rows, :] = jnp.where(first_core, odd, even)
    gram = lax.dot_general(
        factor_a, factor_a, (((1,), (1,)), ((), ())), preferred_element_type=f32
    )
    slab = rank // 4
    blocks = [gram[k * slab : (k + 1) * slab, :] for k in range(4)]
    blank = jnp.zeros((slab, 2 * rank), f32)
    even = jnp.concatenate([blocks[0], blocks[1], blank], axis=1)
    odd = jnp.concatenate([blocks[2], blocks[3], blank], axis=1)
    keep_ref[chunks * rank :, :] = jnp.where(first_core, even, odd)
    send_ref[chunks * rank :, :] = jnp.where(first_core, odd, even)


def send_near_kernel(nears, place_ref, keep_ref, came_ref, own_ref, far_ref, out_ref):
    rank = own_ref.shape[0]
    near_z = WIDE[2]
    first_far = (place_ref[0] // 2) % 2 == 0
    own_b = own_ref[...].astype(f32)
    far_b = far_ref[...].astype(f32)
    low_b = jnp.where(first_far, own_b, far_b).astype(bf16)
    high_b = jnp.where(first_far, far_b, own_b).astype(bf16)
    last = pl.ds(2 * nears * rank, rank // 4)
    gram = keep_ref[last, : 2 * rank] + came_ref[last, : 2 * rank]
    lead = gram.astype(bf16).astype(f32)
    terms = jnp.concatenate([lead, gram - lead], axis=1).astype(bf16)
    for near in range(nears):
        y, z = divmod(near, near_z)
        for far in range(2):
            rows = pl.ds(((y * 2 + far) * near_z + z) * rank, rank)
            out_ref[near, far * rank : (far + 1) * rank, :] = (
                keep_ref[rows, :] + came_ref[rows, :]
            ).astype(bf16)
        out_ref[near, 2 * rank : 3 * rank, :] = low_b
        out_ref[near, 3 * rank : 4 * rank, :] = high_b
        out_ref[near, 4 * rank :, :] = terms


def sum_b_kernel(nears, place_ref, got_ref, a_ref, b_ref, keep_ref, send_ref, factors_ref):
    rank, _ = a_ref.shape
    slab = rank // 4
    first_far = (place_ref[0] // 2) % 2 == 0

    def summed(rows):
        total = got_ref[0, rows, :].astype(f32)
        for near in range(1, nears):
            total = total + got_ref[near, rows, :].astype(f32)
        return total

    low, high = summed(pl.ds(0, rank)), summed(pl.ds(rank, rank))
    terms = summed(pl.ds(4 * rank, slab))
    gram = terms[:, : 2 * rank] + terms[:, 2 * rank :]
    gram = jnp.concatenate([gram, jnp.zeros((slab, LANES - 2 * rank), f32)], axis=1)
    keep_ref[:rank, :] = jnp.where(first_far, low, high)
    send_ref[:rank, :] = jnp.where(first_far, high, low)
    keep_ref[rank:, :] = gram
    send_ref[rank:, :] = gram
    float_a = a_ref[...].astype(f32)
    factors_ref[:, :LANES] = b_ref[...]
    factors_ref[:, LANES:] = jnp.concatenate([float_a, float_a], axis=1).astype(bf16)


def partials_kernel(nears, t_ref, a_ref, ct_ref, both_ref, tile_ref, gram_ref, whole_b):
    rank, i_local = a_ref.shape
    near_z = WIDE[2]
    for core in range(2):
        for near in range(nears):
            y, z = divmod(near, near_z)
            for far in range(2):
                start = (((y * 2 + far) * near_z + z) * 2 + core) * LANES
                whole_b[:, start : start + LANES] = both_ref[
                    core, near, far * rank : (far + 1) * rank, :
                ]
    every_b = whole_b[...]
    contracted = lax.dot_general(
        every_b, t_ref[...], (((1,), (1,)), ((), ())), preferred_element_type=f32
    )
    gram_ref[...] = lax.dot_general(
        every_b, every_b, (((1,), (1,)), ((), ())), preferred_element_type=f32
    )
    first, second = columns_of(ct_ref[...].astype(f32))
    float_a = a_ref[...].astype(f32)
    spot = lane(rank, LANES)
    low_half = spot < i_local
    scaled = contracted * jnp.where(low_half, first, second)
    part_a = scaled + pltpu.roll(scaled, i_local, 1)
    against_a = contracted * jnp.concatenate([float_a, float_a], axis=1)
    c_first = jnp.sum(jnp.where(low_half, against_a, 0.0), axis=1, keepdims=True)
    c_second = jnp.sum(jnp.where(low_half, 0.0, against_a), axis=1, keepdims=True)
    square = lax.broadcasted_iota(jnp.int32, (rank, rank), 0) == lane(rank, rank)
    parts = [jnp.sum(jnp.where(square, c, 0.0), axis=0, keepdims=True) for c in (c_first, c_second)]
    leads = [part.astype(bf16).astype(f32) for part in parts]
    rests = [part - lead for part, lead in zip(parts, leads)]
    own_c = [ct_ref[k : k + 1, :].astype(f32) for k in range(2)]
    half = rank // 2
    tile_ref[:half, :] = jnp.where(lane(half, LANES) < i_local, part_a[:half], part_a[half:])
    tile_ref[half:, :] = jnp.concatenate(
        [
            jnp.concatenate(leads + rests, axis=1),
            jnp.concatenate(own_c + [jnp.zeros((1, 2 * rank), f32)], axis=1),
            jnp.zeros((6, LANES), f32),
        ],
        axis=0,
    )


def send_narrow_kernel(others, keep_ref, came_ref, tile_ref, factors_ref, out_ref):
    rank = factors_ref.shape[1]
    half = rank // 2
    total = keep_ref[...] + came_ref[...]
    gram = total[rank:, : 2 * rank]
    lead = gram.astype(bf16).astype(f32)
    packed = jnp.concatenate(
        [
            total[:rank],
            tile_ref[:half, :],
            jnp.concatenate([lead, gram - lead], axis=1),
            tile_ref[half:, :],
        ],
        axis=0,
    ).astype(bf16)
    for other in range(others):
        out_ref[other] = packed


def residual_kernel(others, links, place_ref, got_ref, factors_ref, gram_b_ref, out_ref, ra_ref, rb_ref, ha_ref, hb_ref, c_ref, model_c_ref, gram_a_ref, gram_c_ref):
    rank, i_local = ra_ref.shape
    k_all = 2 * others
    first_core = place_ref[0] % 2 == 0
    gram_b = gram_b_ref[...]
    half = rank // 2
    slab = rank // 4
    square = lax.broadcasted_iota(jnp.int32, (rank, rank), 0) == lane(rank, rank)
    eye = square.astype(f32)
    spot = lax.broadcasted_iota(jnp.int32, (others, LANES), 0)
    mttkrps = []
    grams = []
    part_c = jnp.zeros((k_all, rank), f32)
    for core in range(2):

        def summed(rows):
            total = got_ref[core, 0, rows, :].astype(f32)
            for other in range(1, others):
                total = total + got_ref[core, other, rows, :].astype(f32)
            return total

        wide_a = summed(pl.ds(rank, half))
        mttkrps.append(
            (
                jnp.concatenate([wide_a[:, :i_local], wide_a[:, i_local:]], axis=0),
                summed(pl.ds(0, rank)),
            )
        )
        gram = got_ref[core, 0, rank + half : rank + half + slab, :].astype(f32)
        gram = gram[:, : 2 * rank] + gram[:, 2 * rank :]
        grams += [gram[:, :rank], gram[:, rank:]]
        upper = jnp.zeros((others, LANES), f32)
        lower = upper
        for other in range(others):
            block = got_ref[core, other, rank + half + slab :, :].astype(f32)
            upper = jnp.where(spot == other, block[0:1, :], upper)
            lower = jnp.where(spot == other, block[1:2, :], lower)
        upper = upper[:, : 2 * rank] + upper[:, 2 * rank :]
        part_c = part_c + jnp.concatenate([upper[:, :rank], upper[:, rank:]], axis=0)
    factor_c = mul_t(eye, jnp.concatenate([lower[:, :rank], lower[:, rank : 2 * rank]], axis=0))
    part_c = mul_t(eye, part_c)
    gram_c = mul_t(factor_c, factor_c)
    gram_a = jnp.concatenate(grams, axis=0)
    had_a = gram_b * gram_c
    had_b = gram_a * gram_c
    gram_a_ref[...] = gram_a
    gram_c_ref[...] = gram_c
    model_c_ref[...] = mul(gram_a * gram_b, factor_c)
    sums = [jnp.zeros((rank, 1), f32)] * 4
    cross_a = jnp.zeros((rank, rank), f32)
    cross_b = cross_a
    kept = []
    for core in range(2):
        float_b = factors_ref[core, :, :LANES].astype(f32)
        float_a = factors_ref[core, :, LANES : LANES + i_local].astype(f32)
        own = []
        for mttkrp, factor, had in (
            (mttkrps[core][0], float_a, had_a),
            (mttkrps[core][1], float_b, had_b),
        ):
            res = mttkrp - mul(had, factor)
            once = mul(had, res)
            twice = mul(had, once)
            own += [res, once]
            pairs = ((res, res), (res, once), (once, once), (once, twice))
            sums = [
                old + jnp.sum(left * right, axis=1, keepdims=True)
                for old, (left, right) in zip(sums, pairs)
            ]
        cross_a = cross_a + mul_t(float_a, own[0])
        cross_b = cross_b + mul_t(float_b, own[2])
        kept.append(own)
    for ref, one, two in zip((ra_ref, ha_ref, rb_ref, hb_ref), *kept):
        ref[...] = jnp.where(first_core, one, two)
    c_ref[...] = factor_c
    last = spread(
        jnp.concatenate(
            [part_c, *sums, jnp.zeros((rank, rank - k_all - len(sums)), f32)], axis=1
        )
    )
    lead = last.astype(bf16).astype(f32)
    cross = jnp.where(first_core, spread(cross_a), spread(cross_b))
    tail = jnp.where(first_core, lead, last - lead)
    packed = jnp.concatenate([cross, tail], axis=0).astype(bf16)
    for link in range(links):
        out_ref[link] = packed


def step_kernel(others, place_ref, all_ref, a_ref, b_ref, gram_a_ref, gram_b_ref, ra_ref, rb_ref, ha_ref, hb_ref, c_ref, model_c_ref, gram_c_ref, sa_ref, sb_ref, sc_ref):
    rank, _ = a_ref.shape
    k_all = 2 * others
    sums = []
    for core in range(2):
        total_sum = all_ref[core, 0].astype(f32)
        for link in range(1, all_ref.shape[1]):
            total_sum = total_sum + all_ref[core, link].astype(f32)
        sums.append(total_sum)
    slab = rank // 4
    cross_a = gather_rows(sums[0][:slab])
    cross_b = gather_rows(sums[1][:slab])
    last = gather_rows(sums[0][slab:] + sums[1][slab:])
    mttkrp_c = last[:, :k_all]
    gram_a = gram_a_ref[...]
    gram_b = gram_b_ref[...]
    factor_c = c_ref[...]
    gram_c = gram_c_ref[...]
    had_a = gram_b * gram_c
    had_b = gram_a * gram_c
    had_c = gram_a * gram_b
    res_c = mttkrp_c - model_c_ref[...]
    once_c = mul(had_c, res_c)
    twice_c = mul(had_c, once_c)
    cross_c = mul_t(factor_c, res_c)

    def total(value):
        return jnp.sum(jnp.sum(value, axis=1, keepdims=True), axis=0, keepdims=True)

    own = [
        total(res_c * res_c),
        total(res_c * once_c),
        total(once_c * once_c),
        total(once_c * twice_c),
    ]
    p0, p1, p2, p3 = [
        total(last[:, k_all + k : k_all + k + 1]) + own[k] for k in range(4)
    ]

    def mixed(xa, xb, xc):
        return (
            xb * gram_c + gram_b * xc,
            xa * gram_c + gram_a * xc,
            xa * gram_b + gram_a * xb,
        )

    eye = (
        lax.broadcasted_iota(jnp.int32, (rank, rank), 0) == lane(rank, rank)
    ).astype(f32)
    grams = (gram_a, gram_b, gram_c)
    shifted = tuple(had + damping * eye for had in (had_a, had_b, had_c))
    crosses = (cross_a, cross_b, cross_c)
    mix = mixed(*crosses)
    mix_gram = [mul(m, g) for m, g in zip(mix, grams)]
    turned = [mul_t(s, x) for s, x in zip(shifted, crosses)]
    twice_turned = [mul(s, t) for s, t in zip(shifted, turned)]
    shifted_mix = [mul(s, m) for s, m in zip(shifted, mix)]
    image_cross_t = [t + mg for t, mg in zip(turned, mix_gram)]
    image_cross = [
        mul(x, s) + mul_t(g, m) for x, s, g, m in zip(crosses, shifted, grams, mix)
    ]
    image_mix = mixed(*image_cross)
    one = damping
    c0 = p0
    k1 = p1 + one * p0
    k2 = p2 + 2.0 * one * p1 + one * one * p0
    k3 = p3 + 3.0 * one * p2 + 3.0 * one * one * p1 + one * one * one * p0
    c1 = k1
    c2 = k2
    c3 = k3
    crosses_t = [mul_t(eye, x) for x in crosses]
    c1 = c1 + total(sum(m * xt for m, xt in zip(mix, crosses_t)))
    c2 = c2 + total(
        sum(2.0 * m * t + mg * m for m, t, mg in zip(mix, turned, mix_gram))
    )
    c3 = c3 + total(
        sum(
            2.0 * m * tt + mg * sm + im * ict
            for m, tt, mg, sm, im, ict in zip(
                mix, twice_turned, mix_gram, shifted_mix, image_mix, image_cross_t
            )
        )
    )
    alpha = c0 / c1
    fresh = c0 - 2.0 * alpha * c1 + alpha * alpha * c2
    beta = fresh / c0
    keep = 1.0 + beta
    curvature = keep * keep * c1 - 2.0 * keep * alpha * c2 + alpha * alpha * c3
    second = fresh / curvature
    on_res = alpha + second * keep
    on_image = -second * alpha
    float_a = a_ref[...].astype(f32)
    float_b = b_ref[...].astype(f32)
    res_a = ra_ref[...]
    res_b = rb_ref[...]
    image_a = damping * res_a + ha_ref[...] + mul(mix[0], float_a)
    image_b = damping * res_b + hb_ref[...] + mul(mix[1], float_b)
    image_c = damping * res_c + once_c + mul(mix[2], factor_c)
    sa_ref[...] = on_res * res_a + on_image * image_a
    sb_ref[...] = on_res * res_b + on_image * image_b
    step_c = on_res * res_c + on_image * image_c
    at = place_ref[0] // 4
    spot = lane(rank, k_all)
    square = lax.broadcasted_iota(jnp.int32, (rank, rank), 0) == lane(rank, rank)
    for k in range(2):
        column = jnp.sum(jnp.where(spot == at + k * others, step_c, 0.0), axis=1, keepdims=True)
        sc_ref[k : k + 1, :] = jnp.sum(jnp.where(square, column, 0.0), axis=0, keepdims=True)


def call(kernel, out_shape, operands, scalar=False, scratch=()):
    vmem = pl.BlockSpec(memory_space=pltpu.VMEM)
    specs = [vmem] * len(operands)
    if scalar:
        specs[0] = pl.BlockSpec(memory_space=pltpu.SMEM)
    outs = out_shape if isinstance(out_shape, tuple) else (out_shape,)
    result = pl.pallas_call(
        kernel,
        out_shape=outs,
        in_specs=specs,
        out_specs=tuple(vmem for _ in outs),
        scratch_shapes=list(scratch),
        compiler_params=pltpu.CompilerParams(vmem_limit_bytes=16 << 20),
    )(*operands)
    return result if isinstance(out_shape, tuple) else result[0]


def stages(tensor, factor_a, factor_b, factor_c):
    k_local, i_local, j_whole = tensor.shape
    rank = factor_a.shape[0]
    chunks = j_whole // (2 * LANES)
    nears = chunks // 2
    others = lax.axis_size(OTHER)
    like = jax.ShapeDtypeStruct
    flattened = tensor.reshape(k_local * i_local, j_whole)
    turned_c = factor_c.T
    place = (
        lax.axis_index("core") + 2 * lax.axis_index("z_far") + 4 * lax.axis_index(OTHER)
    ).astype(jnp.int32).reshape(1)
    half = rank // 2
    square = like((rank, LANES), f32)
    thin = like((rank, i_local), f32)

    slab = rank // 4
    smem = pl.BlockSpec(memory_space=pltpu.SMEM)
    first = pl.pallas_call(
        lead_kernel,
        out_shape=like((8, LANES), f32),
        in_specs=[smem],
        out_specs=pl.BlockSpec(memory_space=pltpu.VMEM),
        cost_estimate=pl.CostEstimate(flops=10_000_000_000, bytes_accessed=8, transcendentals=0),
        compiler_params=pltpu.CompilerParams(vmem_limit_bytes=1 << 20),
    )(place)
    far = lax.ppermute(factor_b, "z_far", [(0, 1), (1, 0)])
    rows = like((chunks * rank + slab, LANES), f32)
    keep, send = call(
        functools.partial(partial_b_kernel, chunks),
        (rows, rows),
        (place, flattened, factor_a, turned_c, first),
        scalar=True,
    )
    came = lax.ppermute(send, "core", [(0, 1), (1, 0)])
    near = call(
        functools.partial(send_near_kernel, nears),
        like((nears, 4 * rank + slab, LANES), bf16),
        (place, keep, came, factor_b, far),
        scalar=True,
    )
    near = lax.all_to_all(near, NEAR, 0, 0, tiled=True)
    rows = like((rank + slab, LANES), f32)
    keep, send, factors = call(
        functools.partial(sum_b_kernel, nears),
        (rows, rows, like((rank, 2 * LANES), bf16)),
        (place, near, factor_a, factor_b),
        scalar=True,
    )
    came = lax.ppermute(send, "z_far", [(0, 1), (1, 0)])
    both = lax.all_gather(near[:, 2 * rank : 4 * rank, :], "core", axis=0, tiled=False)
    tile, gram_b = call(
        functools.partial(partials_kernel, nears),
        (like((half + slab, LANES), f32), like((rank, rank), f32)),
        (flattened, factor_a, turned_c, both),
        scratch=(pltpu.VMEM((rank, j_whole), bf16),),
    )
    factors = lax.all_gather(factors, "core", axis=0, tiled=False)
    narrow = call(
        functools.partial(send_narrow_kernel, others),
        like((others, rank + half + 2 * slab, LANES), bf16),
        (keep, came, tile, factors),
    )
    narrow = lax.all_to_all(narrow, OTHER, 0, 0, tiled=True)
    narrow = lax.all_gather(narrow, "core", axis=0, tiled=False)
    low = like((rank, 2 * others), f32)
    gram = like((rank, rank), f32)
    send, res_a, res_b, once_a, once_b, whole_c, model_c, gram_a, gram_c = call(
        functools.partial(residual_kernel, others, chunks),
        (like((chunks, half, LANES), bf16), thin, square, thin, square, low, low, gram, gram),
        (place, narrow, factors, gram_b),
        scalar=True,
    )
    send = lax.all_to_all(send, LINKS, 0, 0, tiled=True)
    every = lax.all_gather(send, "core", axis=0, tiled=False)
    step_a, step_b, turned_step_c = call(
        functools.partial(step_kernel, others),
        (thin, square, like((k_local, rank), f32)),
        (place, every, factor_a, factor_b, gram_a, gram_b, res_a, res_b, once_a, once_b, whole_c, model_c, gram_c),
        scalar=True,
    )
    return step_a, step_b, turned_step_c.T


def solution(mesh):
    wide = ("y", "z_far", "z_near", "core")
    inner = Mesh(mesh.devices.reshape(WIDE + NARROW), wide + OTHER)
    return jax.shard_map(
        stages,
        mesh=inner,
        in_specs=(P(OTHER, wide, None), P(None, wide), P(None, wide), P(None, OTHER)),
        out_specs=(P(None, wide), P(None, wide), P(None, OTHER)),
        check_vma=False,
    )
```

```python
import functools

import jax
import jax.numpy as jnp
from jax import lax
from jax.experimental import pallas as pl
from jax.experimental.pallas import tpu as pltpu
from jax.sharding import Mesh
from jax.sharding import PartitionSpec as P


f32 = jnp.float32
bf16 = jnp.bfloat16
LANES = 128
damping = 1.0
highest = lax.Precision.HIGHEST

WIDE = (4, 2, 4, 2)
NARROW = (4, 2)
NEAR = ("y", "z_near")
LINKS = ("y", "z_far", "z_near")
OTHER = ("x", "z_hi")


def mul(left, right):
    return jnp.dot(left, right, precision=highest, preferred_element_type=f32)


def mul_t(left, right):
    return lax.dot_general(
        left, right, (((1,), (1,)), ((), ())), precision=highest, preferred_element_type=f32
    )


def lane(rows, width):
    return lax.broadcasted_iota(jnp.int32, (rows, width), 1)


def columns_of(row_block):
    count, rank = row_block.shape
    eye = lax.broadcasted_iota(jnp.int32, (rank, rank), 0) == lane(rank, rank)
    return [
        jnp.sum(jnp.where(eye, row_block[k : k + 1, :], 0.0), axis=1, keepdims=True)
        for k in range(count)
    ]


def spread(square):
    rows = square.shape[0] // 4
    return jnp.concatenate([square[k * rows : (k + 1) * rows, :] for k in range(4)], axis=1)


def gather_rows(wide_block):
    width = wide_block.shape[1] // 4
    return jnp.concatenate([wide_block[:, k * width : (k + 1) * width] for k in range(4)], axis=0)


def lead_kernel(place_ref, out_ref):
    out_ref[...] = jnp.zeros(out_ref.shape, f32) + place_ref[0].astype(f32)


def partial_b_kernel(chunks, place_ref, t_ref, a_ref, ct_ref, first_ref, keep_ref, send_ref):
    rank, _ = a_ref.shape
    factor_a = a_ref[...]
    float_a = factor_a.astype(f32)
    cols = columns_of(ct_ref[...].astype(f32))
    khatri = jnp.concatenate([col * float_a for col in cols], axis=1).astype(bf16)
    pieces = 4
    width = t_ref.shape[1] // pieces
    first_core = place_ref[0] % 2 == 0
    per = width // LANES
    for piece in range(pieces):
        part = jnp.dot(
            khatri, t_ref[:, piece * width : (piece + 1) * width], preferred_element_type=f32
        )
        for step in range(0, per, 2):
            rows = pl.ds((piece * per + step) // 2 * rank, rank)
            even = part[:, step * LANES : (step + 1) * LANES]
            odd = part[:, (step + 1) * LANES : (step + 2) * LANES]
            keep_ref[rows, :] = jnp.where(first_core, even, odd)
            send_ref[rows, :] = jnp.where(first_core, odd, even)
    gram = lax.dot_general(
        factor_a, factor_a, (((1,), (1,)), ((), ())), preferred_element_type=f32
    )
    slab = rank // 4
    blocks = [gram[k * slab : (k + 1) * slab, :] for k in range(4)]
    blank = jnp.zeros((slab, 2 * rank), f32)
    even = jnp.concatenate([blocks[0], blocks[1], blank], axis=1)
    odd = jnp.concatenate([blocks[2], blocks[3], blank], axis=1)
    keep_ref[chunks * rank :, :] = jnp.where(first_core, even, odd)
    send_ref[chunks * rank :, :] = jnp.where(first_core, odd, even)


def send_near_kernel(nears, place_ref, keep_ref, came_ref, own_ref, far_ref, out_ref):
    rank = own_ref.shape[0]
    near_z = WIDE[2]
    first_far = (place_ref[0] // 2) % 2 == 0
    own_b = own_ref[...].astype(f32)
    far_b = far_ref[...].astype(f32)
    low_b = jnp.where(first_far, own_b, far_b).astype(bf16)
    high_b = jnp.where(first_far, far_b, own_b).astype(bf16)
    last = pl.ds(2 * nears * rank, rank // 4)
    gram = keep_ref[last, : 2 * rank] + came_ref[last, : 2 * rank]
    lead = gram.astype(bf16).astype(f32)
    terms = jnp.concatenate([lead, gram - lead], axis=1).astype(bf16)
    for near in range(nears):
        y, z = divmod(near, near_z)
        for far in range(2):
            rows = pl.ds(((y * 2 + far) * near_z + z) * rank, rank)
            out_ref[near, far * rank : (far + 1) * rank, :] = (
                keep_ref[rows, :] + came_ref[rows, :]
            ).astype(bf16)
        out_ref[near, 2 * rank : 3 * rank, :] = low_b
        out_ref[near, 3 * rank : 4 * rank, :] = high_b
        out_ref[near, 4 * rank :, :] = terms


def sum_b_kernel(nears, place_ref, got_ref, a_ref, b_ref, keep_ref, send_ref, factors_ref):
    rank, _ = a_ref.shape
    slab = rank // 4
    first_far = (place_ref[0] // 2) % 2 == 0

    def summed(rows):
        total = got_ref[0, rows, :].astype(f32)
        for near in range(1, nears):
            total = total + got_ref[near, rows, :].astype(f32)
        return total

    low, high = summed(pl.ds(0, rank)), summed(pl.ds(rank, rank))
    terms = summed(pl.ds(4 * rank, slab))
    gram = terms[:, : 2 * rank] + terms[:, 2 * rank :]
    gram = jnp.concatenate([gram, jnp.zeros((slab, LANES - 2 * rank), f32)], axis=1)
    keep_ref[:rank, :] = jnp.where(first_far, low, high)
    send_ref[:rank, :] = jnp.where(first_far, high, low)
    keep_ref[rank:, :] = gram
    send_ref[rank:, :] = gram
    float_a = a_ref[...].astype(f32)
    factors_ref[:, :LANES] = b_ref[...]
    factors_ref[:, LANES:] = jnp.concatenate([float_a, float_a], axis=1).astype(bf16)


def partials_kernel(nears, t_ref, a_ref, ct_ref, both_ref, tile_ref, gram_ref, whole_b):
    rank, i_local = a_ref.shape
    near_z = WIDE[2]
    for core in range(2):
        for near in range(nears):
            y, z = divmod(near, near_z)
            for far in range(2):
                start = (((y * 2 + far) * near_z + z) * 2 + core) * LANES
                whole_b[:, start : start + LANES] = both_ref[
                    core, near, far * rank : (far + 1) * rank, :
                ]
    every_b = whole_b[...]
    contracted = lax.dot_general(
        every_b, t_ref[...], (((1,), (1,)), ((), ())), preferred_element_type=f32
    )
    gram_ref[...] = lax.dot_general(
        every_b, every_b, (((1,), (1,)), ((), ())), preferred_element_type=f32
    )
    first, second = columns_of(ct_ref[...].astype(f32))
    float_a = a_ref[...].astype(f32)
    spot = lane(rank, LANES)
    low_half = spot < i_local
    scaled = contracted * jnp.where(low_half, first, second)
    part_a = scaled + pltpu.roll(scaled, i_local, 1)
    against_a = contracted * jnp.concatenate([float_a, float_a], axis=1)
    c_first = jnp.sum(jnp.where(low_half, against_a, 0.0), axis=1, keepdims=True)
    c_second = jnp.sum(jnp.where(low_half, 0.0, against_a), axis=1, keepdims=True)
    square = lax.broadcasted_iota(jnp.int32, (rank, rank), 0) == lane(rank, rank)
    parts = [jnp.sum(jnp.where(square, c, 0.0), axis=0, keepdims=True) for c in (c_first, c_second)]
    leads = [part.astype(bf16).astype(f32) for part in parts]
    rests = [part - lead for part, lead in zip(parts, leads)]
    own_c = [ct_ref[k : k + 1, :].astype(f32) for k in range(2)]
    half = rank // 2
    tile_ref[:half, :] = jnp.where(lane(half, LANES) < i_local, part_a[:half], part_a[half:])
    tile_ref[half:, :] = jnp.concatenate(
        [
            jnp.concatenate(leads + rests, axis=1),
            jnp.concatenate(own_c + [jnp.zeros((1, 2 * rank), f32)], axis=1),
            jnp.zeros((6, LANES), f32),
        ],
        axis=0,
    )


def send_narrow_kernel(others, place_ref, keep_ref, came_ref, tile_ref, factors_ref, out_ref):
    rank = factors_ref.shape[1]
    half = rank // 2
    total = keep_ref[...] + came_ref[...]
    gram = total[rank:, : 2 * rank]
    lead = gram.astype(bf16).astype(f32)
    terms = jnp.concatenate([lead, gram - lead], axis=1)
    rows = terms.shape[0] // others
    row = lax.broadcasted_iota(jnp.int32, terms.shape, 0)
    at = (place_ref[0] // 4) * rows
    tail = tile_ref[half:, :]
    for k in range(rows):
        share = jnp.sum(jnp.where(row == at + k, terms, 0.0), axis=0, keepdims=True)
        tail = jnp.where(row == 2 + k, share, tail)
    packed = jnp.concatenate([total[:rank], tile_ref[:half, :], tail], axis=0).astype(bf16)
    for other in range(others):
        out_ref[other] = packed


def residual_kernel(others, links, place_ref, got_ref, factors_ref, gram_b_ref, out_ref, ra_ref, rb_ref, ha_ref, hb_ref, c_ref, model_c_ref, gram_a_ref, gram_c_ref):
    rank, i_local = ra_ref.shape
    k_all = 2 * others
    first_core = place_ref[0] % 2 == 0
    gram_b = gram_b_ref[...]
    half = rank // 2
    slab = rank // 4
    square = lax.broadcasted_iota(jnp.int32, (rank, rank), 0) == lane(rank, rank)
    eye = square.astype(f32)
    spot = lax.broadcasted_iota(jnp.int32, (others, LANES), 0)
    mttkrps = []
    grams = []
    part_c = jnp.zeros((k_all, rank), f32)
    for core in range(2):

        def summed(rows):
            total = got_ref[core, 0, rows, :].astype(f32)
            for other in range(1, others):
                total = total + got_ref[core, other, rows, :].astype(f32)
            return total

        wide_a = summed(pl.ds(rank, half))
        mttkrps.append(
            (
                jnp.concatenate([wide_a[:, :i_local], wide_a[:, i_local:]], axis=0),
                summed(pl.ds(0, rank)),
            )
        )
        gram = jnp.zeros((slab, LANES), f32)
        place_of = lax.broadcasted_iota(jnp.int32, (slab, LANES), 0)
        share = slab // others
        upper = jnp.zeros((others, LANES), f32)
        lower = upper
        for other in range(others):
            block = got_ref[core, other, rank + half :, :].astype(f32)
            for k in range(share):
                gram = jnp.where(place_of == other * share + k, block[2 + k : 3 + k, :], gram)
            upper = jnp.where(spot == other, block[0:1, :], upper)
            lower = jnp.where(spot == other, block[1:2, :], lower)
        gram = gram[:, : 2 * rank] + gram[:, 2 * rank :]
        grams += [gram[:, :rank], gram[:, rank:]]
        upper = upper[:, : 2 * rank] + upper[:, 2 * rank :]
        part_c = part_c + jnp.concatenate([upper[:, :rank], upper[:, rank:]], axis=0)
    factor_c = mul_t(eye, jnp.concatenate([lower[:, :rank], lower[:, rank : 2 * rank]], axis=0))
    part_c = mul_t(eye, part_c)
    gram_c = mul_t(factor_c, factor_c)
    gram_a = jnp.concatenate(grams, axis=0)
    had_a = gram_b * gram_c
    had_b = gram_a * gram_c
    gram_a_ref[...] = gram_a
    gram_c_ref[...] = gram_c
    model_c_ref[...] = mul(gram_a * gram_b, factor_c)
    sums = [jnp.zeros((rank, 1), f32)] * 4
    cross_a = jnp.zeros((rank, rank), f32)
    cross_b = cross_a
    kept = []
    for core in range(2):
        float_b = factors_ref[core, :, :LANES].astype(f32)
        float_a = factors_ref[core, :, LANES : LANES + i_local].astype(f32)
        own = []
        for mttkrp, factor, had in (
            (mttkrps[core][0], float_a, had_a),
            (mttkrps[core][1], float_b, had_b),
        ):
            res = mttkrp - mul(had, factor)
            once = mul(had, res)
            twice = mul(had, once)
            own += [res, once]
            pairs = ((res, res), (res, once), (once, once), (once, twice))
            sums = [
                old + jnp.sum(left * right, axis=1, keepdims=True)
                for old, (left, right) in zip(sums, pairs)
            ]
        cross_a = cross_a + mul_t(float_a, own[0])
        cross_b = cross_b + mul_t(float_b, own[2])
        kept.append(own)
    for ref, one, two in zip((ra_ref, ha_ref, rb_ref, hb_ref), *kept):
        ref[...] = jnp.where(first_core, one, two)
    c_ref[...] = factor_c
    last = spread(
        jnp.concatenate(
            [part_c, *sums, jnp.zeros((rank, rank - k_all - len(sums)), f32)], axis=1
        )
    )
    lead = last.astype(bf16).astype(f32)
    cross = jnp.where(first_core, spread(cross_a), spread(cross_b))
    tail = jnp.where(first_core, lead, last - lead)
    packed = jnp.concatenate([cross, tail], axis=0).astype(bf16)
    for link in range(links):
        out_ref[link] = packed


def step_kernel(others, place_ref, all_ref, a_ref, b_ref, gram_a_ref, gram_b_ref, ra_ref, rb_ref, ha_ref, hb_ref, c_ref, model_c_ref, gram_c_ref, sa_ref, sb_ref, sc_ref):
    rank, _ = a_ref.shape
    k_all = 2 * others
    sums = []
    for core in range(2):
        total_sum = all_ref[core, 0].astype(f32)
        for link in range(1, all_ref.shape[1]):
            total_sum = total_sum + all_ref[core, link].astype(f32)
        sums.append(total_sum)
    slab = rank // 4
    cross_a = gather_rows(sums[0][:slab])
    cross_b = gather_rows(sums[1][:slab])
    last = gather_rows(sums[0][slab:] + sums[1][slab:])
    mttkrp_c = last[:, :k_all]
    gram_a = gram_a_ref[...]
    gram_b = gram_b_ref[...]
    factor_c = c_ref[...]
    gram_c = gram_c_ref[...]
    had_a = gram_b * gram_c
    had_b = gram_a * gram_c
    had_c = gram_a * gram_b
    res_c = mttkrp_c - model_c_ref[...]
    once_c = mul(had_c, res_c)
    twice_c = mul(had_c, once_c)
    cross_c = mul_t(factor_c, res_c)

    def total(value):
        return jnp.sum(jnp.sum(value, axis=1, keepdims=True), axis=0, keepdims=True)

    own = [
        total(res_c * res_c),
        total(res_c * once_c),
        total(once_c * once_c),
        total(once_c * twice_c),
    ]
    p0, p1, p2, p3 = [
        total(last[:, k_all + k : k_all + k + 1]) + own[k] for k in range(4)
    ]

    def mixed(xa, xb, xc):
        return (
            xb * gram_c + gram_b * xc,
            xa * gram_c + gram_a * xc,
            xa * gram_b + gram_a * xb,
        )

    eye = (
        lax.broadcasted_iota(jnp.int32, (rank, rank), 0) == lane(rank, rank)
    ).astype(f32)
    grams = (gram_a, gram_b, gram_c)
    shifted = tuple(had + damping * eye for had in (had_a, had_b, had_c))
    crosses = (cross_a, cross_b, cross_c)
    mix = mixed(*crosses)
    mix_gram = [mul(m, g) for m, g in zip(mix, grams)]
    turned = [mul_t(s, x) for s, x in zip(shifted, crosses)]
    twice_turned = [mul(s, t) for s, t in zip(shifted, turned)]
    shifted_mix = [mul(s, m) for s, m in zip(shifted, mix)]
    image_cross_t = [t + mg for t, mg in zip(turned, mix_gram)]
    image_cross = [
        mul(x, s) + mul_t(g, m) for x, s, g, m in zip(crosses, shifted, grams, mix)
    ]
    image_mix = mixed(*image_cross)
    one = damping
    c0 = p0
    k1 = p1 + one * p0
    k2 = p2 + 2.0 * one * p1 + one * one * p0
    k3 = p3 + 3.0 * one * p2 + 3.0 * one * one * p1 + one * one * one * p0
    c1 = k1
    c2 = k2
    c3 = k3
    crosses_t = [mul_t(eye, x) for x in crosses]
    c1 = c1 + total(sum(m * xt for m, xt in zip(mix, crosses_t)))
    c2 = c2 + total(
        sum(2.0 * m * t + mg * m for m, t, mg in zip(mix, turned, mix_gram))
    )
    c3 = c3 + total(
        sum(
            2.0 * m * tt + mg * sm + im * ict
            for m, tt, mg, sm, im, ict in zip(
                mix, twice_turned, mix_gram, shifted_mix, image_mix, image_cross_t
            )
        )
    )
    alpha = c0 / c1
    fresh = c0 - 2.0 * alpha * c1 + alpha * alpha * c2
    beta = fresh / c0
    keep = 1.0 + beta
    curvature = keep * keep * c1 - 2.0 * keep * alpha * c2 + alpha * alpha * c3
    second = fresh / curvature
    on_res = alpha + second * keep
    on_image = -second * alpha
    float_a = a_ref[...].astype(f32)
    float_b = b_ref[...].astype(f32)
    res_a = ra_ref[...]
    res_b = rb_ref[...]
    image_a = damping * res_a + ha_ref[...] + mul(mix[0], float_a)
    image_b = damping * res_b + hb_ref[...] + mul(mix[1], float_b)
    image_c = damping * res_c + once_c + mul(mix[2], factor_c)
    sa_ref[...] = on_res * res_a + on_image * image_a
    sb_ref[...] = on_res * res_b + on_image * image_b
    step_c = on_res * res_c + on_image * image_c
    at = place_ref[0] // 4
    spot = lane(rank, k_all)
    square = lax.broadcasted_iota(jnp.int32, (rank, rank), 0) == lane(rank, rank)
    for k in range(2):
        column = jnp.sum(jnp.where(spot == at + k * others, step_c, 0.0), axis=1, keepdims=True)
        sc_ref[k : k + 1, :] = jnp.sum(jnp.where(square, column, 0.0), axis=0, keepdims=True)


def call(kernel, out_shape, operands, scalar=False, scratch=()):
    vmem = pl.BlockSpec(memory_space=pltpu.VMEM)
    specs = [vmem] * len(operands)
    if scalar:
        specs[0] = pl.BlockSpec(memory_space=pltpu.SMEM)
    outs = out_shape if isinstance(out_shape, tuple) else (out_shape,)
    result = pl.pallas_call(
        kernel,
        out_shape=outs,
        in_specs=specs,
        out_specs=tuple(vmem for _ in outs),
        scratch_shapes=list(scratch),
        compiler_params=pltpu.CompilerParams(vmem_limit_bytes=16 << 20),
    )(*operands)
    return result if isinstance(out_shape, tuple) else result[0]


def stages(tensor, factor_a, factor_b, factor_c):
    k_local, i_local, j_whole = tensor.shape
    rank = factor_a.shape[0]
    chunks = j_whole // (2 * LANES)
    nears = chunks // 2
    others = lax.axis_size(OTHER)
    like = jax.ShapeDtypeStruct
    flattened = tensor.reshape(k_local * i_local, j_whole)
    turned_c = factor_c.T
    place = (
        lax.axis_index("core") + 2 * lax.axis_index("z_far") + 4 * lax.axis_index(OTHER)
    ).astype(jnp.int32).reshape(1)
    half = rank // 2
    square = like((rank, LANES), f32)
    thin = like((rank, i_local), f32)

    slab = rank // 4
    smem = pl.BlockSpec(memory_space=pltpu.SMEM)
    first = pl.pallas_call(
        lead_kernel,
        out_shape=like((8, LANES), f32),
        in_specs=[smem],
        out_specs=pl.BlockSpec(memory_space=pltpu.VMEM),
        cost_estimate=pl.CostEstimate(flops=10_000_000_000, bytes_accessed=8, transcendentals=0),
        compiler_params=pltpu.CompilerParams(vmem_limit_bytes=1 << 20),
    )(place)
    far = lax.ppermute(factor_b, "z_far", [(0, 1), (1, 0)])
    rows = like((chunks * rank + slab, LANES), f32)
    keep, send = call(
        functools.partial(partial_b_kernel, chunks),
        (rows, rows),
        (place, flattened, factor_a, turned_c, first),
        scalar=True,
    )
    came = lax.ppermute(send, "core", [(0, 1), (1, 0)])
    near = call(
        functools.partial(send_near_kernel, nears),
        like((nears, 4 * rank + slab, LANES), bf16),
        (place, keep, came, factor_b, far),
        scalar=True,
    )
    near = lax.all_to_all(near, NEAR, 0, 0, tiled=True)
    rows = like((rank + slab, LANES), f32)
    keep, send, factors = call(
        functools.partial(sum_b_kernel, nears),
        (rows, rows, like((rank, 2 * LANES), bf16)),
        (place, near, factor_a, factor_b),
        scalar=True,
    )
    came = lax.ppermute(send, "z_far", [(0, 1), (1, 0)])
    both = lax.all_gather(near[:, 2 * rank : 4 * rank, :], "core", axis=0, tiled=False)
    tile, gram_b = call(
        functools.partial(partials_kernel, nears),
        (like((half + slab, LANES), f32), like((rank, rank), f32)),
        (flattened, factor_a, turned_c, both),
        scratch=(pltpu.VMEM((rank, j_whole), bf16),),
    )
    factors = lax.all_gather(factors, "core", axis=0, tiled=False)
    narrow = call(
        functools.partial(send_narrow_kernel, others),
        like((others, rank + half + slab, LANES), bf16),
        (place, keep, came, tile, factors),
        scalar=True,
    )
    narrow = lax.all_to_all(narrow, OTHER, 0, 0, tiled=True)
    narrow = lax.all_gather(narrow, "core", axis=0, tiled=False)
    low = like((rank, 2 * others), f32)
    gram = like((rank, rank), f32)
    send, res_a, res_b, once_a, once_b, whole_c, model_c, gram_a, gram_c = call(
        functools.partial(residual_kernel, others, chunks),
        (like((chunks, half, LANES), bf16), thin, square, thin, square, low, low, gram, gram),
        (place, narrow, factors, gram_b),
        scalar=True,
    )
    send = lax.all_to_all(send, LINKS, 0, 0, tiled=True)
    every = lax.all_gather(send, "core", axis=0, tiled=False)
    step_a, step_b, turned_step_c = call(
        functools.partial(step_kernel, others),
        (thin, square, like((k_local, rank), f32)),
        (place, every, factor_a, factor_b, gram_a, gram_b, res_a, res_b, once_a, once_b, whole_c, model_c, gram_c),
        scalar=True,
    )
    return step_a, step_b, turned_step_c.T


def solution(mesh):
    wide = ("y", "z_far", "z_near", "core")
    inner = Mesh(mesh.devices.reshape(WIDE + NARROW), wide + OTHER)
    return jax.shard_map(
        stages,
        mesh=inner,
        in_specs=(P(OTHER, wide, None), P(None, wide), P(None, wide), P(None, OTHER)),
        out_specs=(P(None, wide), P(None, wide), P(None, OTHER)),
        check_vma=False,
    )
```
